256 devices in a mesh: gx: 128 (over z, x, y), sa: 2 (over core).
Axes of the slice: x: 4, y: 4, z: 8, core: 2. Of those that a mesh axis runs over, the one named last changes fastest.
Arguments:
- inputs: bfloat16 [2, 16, 512, 128, 128], P('sa', None, 'gx'), may hold values from -6 to 6
- preact: bfloat16 [2, 16, 512, 128, 128], P('sa', None, 'gx'), may hold values from -6 to 6
- cotangent: bfloat16 [2, 16, 512, 128, 128], P('sa', None, 'gx'), may hold values from -6 to 6
- mode_weight: bfloat16 [16, 16, 2048, 128], P(None, None, 'gx'), may hold values from -1 to 1
- bypass_weight: bfloat16 [16, 16], replicated, may hold values from -1.5 to 1.5
Outputs:
- input_grad: bfloat16 [2, 16, 512, 128, 128], P('sa', None, 'gx')
- mode_grad: float32 [16, 16, 2048, 128], P(None, None, ('gx', 'sa'))
The draws below stay inside these ranges and needn't reach their ends.
All inputs are finite; a program needn't handle non-finite values.
Results may differ from the reference program's by a relative error of at most 0.0097.
Values may be sent and summed in bfloat16 or wider, within the bound.
No kernel may reach another device: no remote copies, remote signals or barrier semaphores. Data moves between devices by JAX's collectives and lax.ppermute only.
A program may use at most 128 MiB of HBM per device.

```python
import math
import jax
import jax.numpy as jnp
from jax import lax

C = 16
SY = 128
ST = 128
MX = 64
MY = 64
MT = 32
X = 512
PAIRS = 2048
NS = 2


def block_levels(stream_key, extent, shards, least, high):
    def one(dim, blocks):
        draws = jax.random.uniform(jax.random.fold_in(jax.random.fold_in(stream_key, 6), dim), (blocks,), jnp.float32, least / len(shards), high / len(shards))
        return jnp.repeat(jnp.exp(draws), extent[dim] // blocks).reshape((-1,) + (1,) * (len(extent) - dim - 1))

    gain = one(*shards[0])
    for cut in shards[1:]:
        gain = gain * one(*cut)
    return gain


def noise(own_key, extent, scale, reach, shards=(), kind=jnp.bfloat16):
    loudness = block_levels(own_key, extent, shards, -0.22, 0.18) if shards else 1.0
    array = jax.random.normal(own_key, extent, jnp.float32) * scale * loudness
    return jnp.minimum(jnp.maximum(array, -reach), reach).astype(kind)


def setup_inputs(seed: int = 0) -> dict:
    splits = jax.random.split(jax.random.key(seed), 6)
    inputs = noise(splits[0], (NS, C, X, SY, ST), 1.0, 6.0, ((0, 2), (2, 128)))
    preact = noise(splits[1], (NS, C, X, SY, ST), 1.5, 6.0, ((0, 2), (2, 128)))
    cotangent = noise(splits[2], (NS, C, X, SY, ST), 1.0, 6.0, ((0, 2), (2, 128)))
    mode_weight = noise(splits[3], (C, C, PAIRS, 2 * MX), (2 * C) ** -0.5, 1.0, ((2, 128),))
    bypass_weight = noise(splits[4], (C, C), C ** -0.5, 1.5)
    return {"inputs": inputs, "preact": preact, "cotangent": cotangent, "mode_weight": mode_weight, "bypass_weight": bypass_weight}


root_half = math.sqrt(0.5)
gauss_norm = 1.0 / math.sqrt(2.0 * math.pi)

def tables(kept_count, length, two_sided):
    frequency = jnp.arange(kept_count, dtype=jnp.int32)
    if two_sided:
        frequency = jnp.where(frequency < kept_count // 2, frequency, frequency + (length - kept_count))
    position = jnp.arange(length, dtype=jnp.int32)
    product = frequency[:, None] * position[None, :] % length
    phase_angle = product.astype(jnp.float32) * (2.0 * math.pi / length)
    return (jnp.cos(phase_angle).astype(jnp.bfloat16), jnp.sin(phase_angle).astype(jnp.bfloat16))

def gelu_backward(pieces):
    values = pieces[0].astype(jnp.float32)
    slope = 0.5 * (1.0 + jax.scipy.special.erf(values * root_half)) + values * jnp.exp(-0.5 * values * values) * gauss_norm
    return (pieces[1].astype(jnp.float32) * slope).astype(jnp.bfloat16)

def gradient_term(input_hat, grad_hat, half):
    input_real = input_hat[..., :half].astype(jnp.float32)[:, None]
    input_imag = input_hat[..., half:].astype(jnp.float32)[:, None]
    grad_real = grad_hat[..., :half].astype(jnp.float32)[None]
    grad_imag = grad_hat[..., half:].astype(jnp.float32)[None]
    return jnp.concatenate([input_real * grad_real + input_imag * grad_imag, input_real * grad_imag - input_imag * grad_real], axis=-1)

def reference(inputs, preact, cotangent, mode_weight, bypass_weight):
    pair_count = MY * MT
    cell_count = X * SY * ST
    scale_in = float(MX * pair_count * cell_count) ** (-0.25)
    scale_out = float(cell_count) ** (-0.5)
    cosine_time, sine_time = tables(MT, ST, False)
    cosine_y, sine_y = tables(MY, SY, True)
    cosine_x, sine_x = tables(MX, X, True)
    forward_time = jnp.concatenate([cosine_time.T, -sine_time.T], axis=1)
    inverse_time = jnp.concatenate([cosine_time, -sine_time], axis=0)
    plane_table = jnp.stack([jnp.stack([cosine_y, sine_y], -1), jnp.stack([-sine_y, cosine_y], -1)]).astype(jnp.float32)
    x_forward = jnp.stack([jnp.concatenate([cosine_x, -sine_x], 0).T, jnp.concatenate([sine_x, cosine_x], 0).T], 1).astype(jnp.float32)
    x_inverse = jnp.stack([jnp.concatenate([cosine_x, -sine_x], 0), jnp.concatenate([sine_x, cosine_x], 0)], -1).astype(jnp.float32)

    def forward_field(field):
        sectioned = jnp.dot(field.reshape(-1, ST), forward_time, preferred_element_type=jnp.float32).astype(jnp.bfloat16)
        sectioned = sectioned.reshape(X, SY, 2, MT).astype(jnp.float32)
        plane = jnp.einsum('xyqk,ajyq->xajk', sectioned, plane_table).astype(jnp.bfloat16)
        plane = plane.reshape(X, 2, pair_count).astype(jnp.float32)
        return jnp.einsum('xqp,xqr->pr', plane, x_forward)

    def scaled_input(field):
        return (scale_in * forward_field(field)).astype(jnp.bfloat16)

    def scaled_grad(field):
        return (scale_out * forward_field(field)).astype(jnp.bfloat16)
    grad_total = jnp.zeros((C, C, pair_count, 2 * MX), jnp.float32)
    results = []
    for sample in range(NS):
        dz_field = lax.map(gelu_backward, (preact[sample], cotangent[sample]))
        input_hat = lax.map(scaled_input, inputs[sample])
        grad_hat = lax.map(scaled_grad, dz_field)
        grad_total = grad_total + gradient_term(input_hat, grad_hat, MX)
        grad_real = grad_hat[..., :MX].astype(jnp.float32)
        grad_imag = grad_hat[..., MX:].astype(jnp.float32)

        def adjoint_row(weight_row):
            weights = weight_row.astype(jnp.float32)
            real_part = lax.optimization_barrier(jnp.sum(weights[..., :MX] * grad_real + weights[..., MX:] * grad_imag, axis=0))
            imag_part = lax.optimization_barrier(jnp.sum(weights[..., :MX] * grad_imag - weights[..., MX:] * grad_real, axis=0))
            return jnp.concatenate([real_part, imag_part], axis=-1).astype(jnp.bfloat16)
        back_hat = lax.map(adjoint_row, mode_weight)

        def inverse_field(pieces):
            back_block, bypass_row = pieces
            grid_rows = jnp.einsum('pr,rxq->xqp', back_block.astype(jnp.float32), x_inverse).astype(jnp.bfloat16)
            grid_rows = grid_rows.reshape(X, 2, MY, MT).astype(jnp.float32)
            joined = jnp.einsum('xajk,ajyq->xyqk', grid_rows, plane_table).astype(jnp.bfloat16)
            spectral = jnp.dot(joined.reshape(-1, 2 * MT), inverse_time, preferred_element_type=jnp.float32)
            spectral = spectral.reshape(X, SY, ST)
            bypass = jnp.dot(bypass_row[None, :], dz_field.reshape(C, -1), preferred_element_type=jnp.float32).reshape(X, SY, ST)
            return (scale_in * spectral + bypass).astype(jnp.bfloat16)
        results.append(lax.map(inverse_field, (back_hat, bypass_weight)))
    return (jnp.stack(results), grad_total)
```

```python
import math

import jax
import jax.numpy as jnp
import numpy as np
from jax import lax
from jax.experimental import pallas as pl
from jax.experimental.pallas import tpu as pltpu
from jax.sharding import PartitionSpec as P

MY = 64
MT = 32

root_half = math.sqrt(0.5)
gauss_norm = 1.0 / math.sqrt(2.0 * math.pi)
f32 = jnp.float32
bf16 = jnp.bfloat16


def tables(kept_count, length, two_sided):
    frequency = np.arange(kept_count)
    if two_sided:
        frequency = np.where(
            frequency < kept_count // 2, frequency, frequency + (length - kept_count)
        )
    product = frequency[:, None] * np.arange(length)[None, :] % length
    phase_angle = product * (2.0 * math.pi / length)
    return (
        np.cos(phase_angle).astype(np.float32).astype(bf16).astype(np.float32),
        np.sin(phase_angle).astype(np.float32).astype(bf16).astype(np.float32),
    )


def constants(cells_x, cells_y, cells_time, modes_x, slab):
    ct, st = tables(MT, cells_time, False)
    cy, sy = tables(MY, cells_y, True)
    cx, sx = tables(modes_x, cells_x, True)
    four = np.eye(4, dtype=np.float32)
    time = np.stack([ct, -st]).reshape(2, 2, MT // 2, cells_time)
    time_forward = np.einsum("cd,qhkt->ctqhdk", four, time).reshape(4 * cells_time, -1)
    time_inverse = np.einsum("cd,qhkt->qhckdt", four, time).reshape(-1, 4 * cells_time)
    plane = np.block([[cy, sy], [-sy, cy]])
    x_forward = np.stack([np.concatenate([cx, -sx]).T, np.concatenate([sx, cx]).T], 1)
    devices = cells_x // slab
    both = np.einsum(
        "fg,dvr->frdgv", np.eye(2, dtype=np.float32), x_forward.reshape(devices, 2 * slab, -1)
    ).reshape(2 * 2 * modes_x, -1)
    x_inverse = np.stack([np.concatenate([cx, -sx]), np.concatenate([sx, cx])], -1)
    x_inverse = x_inverse.reshape(2 * modes_x, -1).T
    return [
        a.astype(bf16) for a in (time_forward, time_inverse, plane, plane.T, both, x_inverse)
    ]


def low_lanes(shape):
    return lax.broadcasted_iota(jnp.int32, shape, len(shape) - 1) < 64


def gelu_backward(values, cotangent):
    slope = (
        0.5 * (1.0 + lax.erf(values * root_half))
        + values * jnp.exp(-0.5 * values * values) * gauss_norm
    )
    return cotangent * slope


def forward_kernel(pre_ref, cot_ref, inp_ref, time_ref, plane_ref, send_ref, dz_ref, acc0, acc1):
    x = pl.program_id(0)
    for c in range(16):
        dz_ref[c] = gelu_backward(pre_ref[c].astype(f32), cot_ref[c].astype(f32)).astype(bf16)
    low = low_lanes((128, 128))
    for field, ref in enumerate((dz_ref, inp_ref)):
        rows = jnp.concatenate(
            [jnp.concatenate([ref[4 * g + c] for c in range(4)], axis=1) for g in range(4)], axis=0
        )
        sect = jnp.dot(rows, time_ref[...], preferred_element_type=f32).astype(bf16)
        stacked = jnp.concatenate(
            [
                jnp.concatenate(
                    [sect[128 * g : 128 * g + 128, 128 * q : 128 * q + 128] for g in range(4)],
                    axis=1,
                )
                for q in range(2)
            ],
            axis=0,
        )
        plane = jnp.dot(plane_ref[...], stacked, preferred_element_type=f32)
        for pair, acc in enumerate((acc0, acc1)):
            first = plane[:, 256 * pair : 256 * pair + 128]
            second = plane[:, 256 * pair + 128 : 256 * pair + 256]
            halves = (
                jnp.where(low, first, pltpu.roll(second, 64, 1)),
                jnp.where(low, pltpu.roll(first, 64, 1), second),
            )
            for h in range(2):
                for a in range(2):
                    start = h * 16 + field * 8 + a + 2 * x
                    acc[pl.ds(start, 64, stride=32), :] = halves[h][64 * a : 64 * a + 64]

    @pl.when(x == 3)
    def _():
        send_ref[:, :, 0:128] = acc0[...].reshape(128, 16, 128).astype(bf16)
        send_ref[:, :, 128:256] = acc1[...].reshape(128, 16, 128).astype(bf16)


def middle_kernel(scale_in, scale_out):
    def kernel(core_ref, recv_ref, xf_ref, w_ref, xi_ref, send_ref, mine_ref, other_ref, back_ref, g_ref, gr_ref):
        core = core_ref[0]
        block = recv_ref[...].reshape(2048, 256)
        summed = jnp.dot(xf_ref[...], block, preferred_element_type=f32).T
        hats = jnp.concatenate([summed[:, :128] * scale_out, summed[:, 128:] * scale_in], axis=1)
        hats = hats.astype(bf16).astype(f32)
        grad = hats[:, :128]
        g_ref[0] = grad
        g_ref[1] = hats[:, 128:]
        gr_ref[...] = pltpu.roll(grad, 64, 1)
        for f in range(2):
            for c in range(16):
                mine_ref[f, c] = g_ref[f, pl.ds(16 * c + 8 * core, 8), :].astype(bf16)
                other_ref[f, c] = g_ref[f, pl.ds(16 * c + 8 - 8 * core, 8), :].astype(bf16)
        low = low_lanes((16, 128))
        for i in range(16):
            same = jnp.zeros((16, 128), f32)
            cross = jnp.zeros((16, 128), f32)
            for o in range(16):
                weight = w_ref[i, o].astype(f32)
                same = same + weight * g_ref[0, 16 * o : 16 * o + 16, :]
                cross = cross + weight * gr_ref[16 * o : 16 * o + 16, :]
            back = jnp.where(low, same + pltpu.roll(same, 64, 1), pltpu.roll(cross, 64, 1) - cross)
            back_ref[16 * i : 16 * i + 16, :] = back.astype(bf16)
        grid_rows = lax.dot_general(
            xi_ref[...], back_ref[...], (((1,), (1,)), ((), ())), preferred_element_type=f32
        )
        send_ref[...] = grid_rows.reshape(128, 8, 256).astype(bf16)

    return kernel


def mode_kernel(mine_ref, other_ref, out_ref, g_ref, gx_ref):
    low = low_lanes((16, 8, 128))
    for s, ref in enumerate((mine_ref, other_ref)):
        grad = ref[0].astype(f32)
        rolled = pltpu.roll(grad, 64, 2)
        g_ref[s] = grad
        gx_ref[s] = jnp.where(low, rolled, -rolled)
    low = low_lanes((8, 128))
    for i in range(16):
        real, imag = [], []
        for ref in (mine_ref, other_ref):
            value = ref[1, i].astype(f32)
            rolled = pltpu.roll(value, 64, 1)
            real.append(jnp.where(low, value, rolled))
            imag.append(jnp.where(low, rolled, value))
        for o in range(16):
            out_ref[i, o] = (
                real[0] * g_ref[0, o]
                + imag[0] * gx_ref[0, o]
                + (real[1] * g_ref[1, o] + imag[1] * gx_ref[1, o])
            )


def bypass_kernel(b_ref, dz_ref, out_ref):
    row = lax.broadcasted_iota(jnp.int32, (256, 16), 0)
    col = lax.broadcasted_iota(jnp.int32, (256, 16), 1)
    spread = jnp.where(row // 16 == col, 1.0, 0.0).astype(bf16)
    left = jnp.dot(spread, b_ref[...], preferred_element_type=f32).astype(bf16)
    full = lax.dot_general(left, spread, (((1,), (1,)), ((), ())), preferred_element_type=f32)
    row = lax.broadcasted_iota(jnp.int32, (256, 256), 0)
    col = lax.broadcasted_iota(jnp.int32, (256, 256), 1)
    mix = jnp.where(row % 16 == col % 16, full, 0.0).astype(bf16)
    rows = jnp.concatenate(
        [
            jnp.concatenate([dz_ref[o, 16 * b : 16 * b + 16, :] for o in range(16)], axis=0)
            for b in range(8)
        ],
        axis=1,
    )
    mixed = jnp.dot(mix, rows, preferred_element_type=f32)
    for i in range(16):
        for b in range(8):
            out_ref[i, 16 * b : 16 * b + 16, :] = mixed[
                16 * i : 16 * i + 16, 128 * b : 128 * b + 128
            ]


def inverse_kernel(scale_in):
    def kernel(recv_ref, plane_ref, time_ref, bypass_ref, out_ref, rows_ref):
        x = pl.program_id(0)

        @pl.when(x == 0)
        def _():
            block = recv_ref[...].astype(f32).reshape(64, 2, 8, 256)
            low = low_lanes((512, 128))
            for v in range(2):
                first = block[:, 0, :, 128 * v : 128 * v + 128].reshape(512, 128)
                second = block[:, 1, :, 128 * v : 128 * v + 128].reshape(512, 128)
                rows_ref[2 * v] = jnp.where(low, first, pltpu.roll(second, 64, 1))
                rows_ref[2 * v + 1] = jnp.where(low, pltpu.roll(first, 64, 1), second)

        spectra = jnp.concatenate(
            [
                jnp.concatenate(
                    [rows_ref[g, pl.ds(2 * x + a, 64, stride=8), :] for a in range(2)], axis=0
                )
                for g in range(4)
            ],
            axis=1,
        ).astype(bf16)
        joined = jnp.dot(plane_ref[...], spectra, preferred_element_type=f32).astype(bf16)
        stacked = jnp.concatenate(
            [
                jnp.concatenate(
                    [joined[128 * q : 128 * q + 128, 128 * g : 128 * g + 128] for q in range(2)],
                    axis=1,
                )
                for g in range(4)
            ],
            axis=0,
        )
        spectral = jnp.dot(stacked, time_ref[...], preferred_element_type=f32)
        for g in range(4):
            for c in range(4):
                out_ref[4 * g + c] = (
                    scale_in * spectral[128 * g : 128 * g + 128, 128 * c : 128 * c + 128]
                    + bypass_ref[4 * g + c]
                ).astype(bf16)

    return kernel


def whole(*shape):
    return pl.BlockSpec(shape, lambda *_: (0,) * len(shape))


def per_cell():
    return pl.BlockSpec((16, None, 128, 128), lambda x: (0, x, 0, 0))


def shards(inputs, preact, cotangent, mode_weight, bypass_weight):
    slab = inputs.shape[2]
    cells_y = inputs.shape[3]
    cells_time = inputs.shape[4]
    cells_x = slab * lax.axis_size("gx")
    modes_x = mode_weight.shape[3] // 2
    cell_count = cells_x * cells_y * cells_time
    scale_in = float(modes_x * MY * MT * cell_count) ** (-0.25)
    scale_out = float(cell_count) ** (-0.5)
    time_forward, time_inverse, plane, plane_back, x_forward, x_inverse = constants(
        cells_x, cells_y, cells_time, modes_x, slab
    )
    core = lax.axis_index("sa").astype(jnp.int32).reshape(1)

    send, dz = pl.pallas_call(
        forward_kernel,
        grid=(4,),
        in_specs=[per_cell(), per_cell(), per_cell(), whole(512, 256), whole(128, 256)],
        out_specs=[whole(128, 16, 256), per_cell()],
        out_shape=[
            jax.ShapeDtypeStruct((128, 16, 256), bf16),
            jax.ShapeDtypeStruct((16, 4, 128, 128), bf16),
        ],
        scratch_shapes=[pltpu.VMEM((2048, 128), f32), pltpu.VMEM((2048, 128), f32)],
        name="forward",
    )(preact[0], cotangent[0], inputs[0], time_forward, plane)
    recv = lax.all_to_all(send, "gx", split_axis=0, concat_axis=0, tiled=True)
    bypass = pl.pallas_call(
        bypass_kernel,
        grid=(4,),
        in_specs=[whole(16, 16), per_cell()],
        out_specs=per_cell(),
        out_shape=jax.ShapeDtypeStruct((16, 4, 128, 128), f32),
        name="bypass",
    )(bypass_weight, dz)
    rows, mine, other = pl.pallas_call(
        middle_kernel(scale_in, scale_out),
        in_specs=[pl.BlockSpec(memory_space=pltpu.SMEM)]
        + [pl.BlockSpec(memory_space=pltpu.VMEM)] * 4,
        out_specs=[pl.BlockSpec(memory_space=pltpu.VMEM)] * 3,
        out_shape=[
            jax.ShapeDtypeStruct((128, 8, 256), bf16),
            jax.ShapeDtypeStruct((2, 16, 8, 128), bf16),
            jax.ShapeDtypeStruct((2, 16, 8, 128), bf16),
        ],
        scratch_shapes=[
            pltpu.VMEM((256, 128), bf16),
            pltpu.VMEM((2, 256, 128), f32),
            pltpu.VMEM((256, 128), f32),
        ],
        name="middle",
    )(core, recv, x_forward, mode_weight, x_inverse)
    back = lax.all_to_all(rows, "gx", split_axis=0, concat_axis=0, tiled=True)
    theirs = lax.ppermute(other, "sa", [(0, 1), (1, 0)])
    mode_grad = pl.pallas_call(
        mode_kernel,
        out_shape=jax.ShapeDtypeStruct((16, 16, 8, 128), f32),
        scratch_shapes=[pltpu.VMEM((2, 16, 8, 128), f32), pltpu.VMEM((2, 16, 8, 128), f32)],
        name="modes",
    )(mine, theirs)
    input_grad = pl.pallas_call(
        inverse_kernel(scale_in),
        grid=(4,),
        in_specs=[whole(128, 8, 256), whole(256, 128), whole(256, 512), per_cell()],
        out_specs=per_cell(),
        out_shape=jax.ShapeDtypeStruct((16, 4, 128, 128), bf16),
        scratch_shapes=[pltpu.VMEM((4, 512, 128), f32)],
        name="inverse",
    )(back, plane_back, time_inverse, bypass)
    return (input_grad[None], mode_grad)


def solution(mesh):
    field = P("sa", None, "gx", None, None)
    return jax.shard_map(
        shards,
        mesh=mesh,
        in_specs=(field, field, field, P(None, None, "gx", None), P()),
        out_specs=(field, P(None, None, ("gx", "sa"), None)),
        check_vma=False,
    )
```

```python
import math

import jax
import jax.numpy as jnp
import numpy as np
from jax import lax
from jax.experimental import pallas as pl
from jax.experimental.pallas import tpu as pltpu
from jax.sharding import PartitionSpec as P

MY = 64
MT = 32

root_half = math.sqrt(0.5)
gauss_norm = 1.0 / math.sqrt(2.0 * math.pi)
f32 = jnp.float32
bf16 = jnp.bfloat16


def tables(kept_count, length, two_sided):
    frequency = np.arange(kept_count)
    if two_sided:
        frequency = np.where(
            frequency < kept_count // 2, frequency, frequency + (length - kept_count)
        )
    product = frequency[:, None] * np.arange(length)[None, :] % length
    phase_angle = product * (2.0 * math.pi / length)
    return (
        np.cos(phase_angle).astype(np.float32).astype(bf16).astype(np.float32),
        np.sin(phase_angle).astype(np.float32).astype(bf16).astype(np.float32),
    )


def constants(cells_x, cells_y, cells_time, modes_x, slab):
    ct, st = tables(MT, cells_time, False)
    cy, sy = tables(MY, cells_y, True)
    cx, sx = tables(modes_x, cells_x, True)
    four = np.eye(4, dtype=np.float32)
    time = np.stack([ct, -st]).reshape(2, 2, MT // 2, cells_time)
    time_forward = np.einsum("cd,qhkt->ctqhdk", four, time).reshape(4 * cells_time, -1)
    time_inverse = np.einsum("cd,qhkt->qhckdt", four, time).reshape(-1, 4 * cells_time)
    plane = np.block([[cy, sy], [-sy, cy]])
    plane_rows = plane.reshape(2, MY, 1, -1).repeat(slab, 2).transpose(1, 2, 0, 3)
    plane_rows = plane_rows.reshape(MY * slab * 2, -1)
    line = np.stack([np.concatenate([cx, -sx]), np.concatenate([sx, cx])], -1)
    line = line.reshape(2 * modes_x, -1).T
    return [
        a.astype(bf16) for a in (time_forward, time_inverse, plane_rows, plane.T, line)
    ]


def low_lanes(shape):
    return lax.broadcasted_iota(jnp.int32, shape, len(shape) - 1) < 64


def gelu_backward(values, cotangent):
    scaled = values * root_half
    density = jnp.exp2((scaled * scaled) * -math.log2(math.e))
    slope = (1.0 + lax.erf(scaled)) + (scaled * (4.0 * root_half * gauss_norm)) * density
    return (cotangent * 0.5) * slope


def forward_kernel(
    pre_hbm,
    cot_hbm,
    inp_hbm,
    time_hbm,
    plane_hbm,
    send_hbm,
    dz_ref,
    pre_ref,
    cot_ref,
    inp_ref,
    time_ref,
    plane_ref,
    send_ref,
    table_ref,
    sect_ref,
    half_ref,
    sems,
    table_sems,
    sent,
):
    plane_copy = pltpu.make_async_copy(plane_hbm, plane_ref, table_sems.at[0])
    time_copy = pltpu.make_async_copy(time_hbm, time_ref, table_sems.at[1])
    plane_copy.start()
    time_copy.start()
    copies = []
    for g in range(4):
        part = pl.ds(4 * g, 4)
        trio = [
            pltpu.make_async_copy(src.at[part], dst.at[part], sems.at[n, g])
            for n, (src, dst) in enumerate(
                ((inp_hbm, inp_ref), (pre_hbm, pre_ref), (cot_hbm, cot_ref))
            )
        ]
        for copy in trio:
            copy.start()
        copies.append(trio)
    row_x = lax.broadcasted_iota(jnp.int32, (512, 256), 0) // 2 % 4
    plane_copy.wait()
    plane = plane_ref[...].astype(f32)
    for x in range(4):
        table_ref[:, 256 * x : 256 * x + 256] = jnp.where(row_x == x, plane, 0.0).astype(bf16)
    low = low_lanes((512, 128))
    time_copy.wait()

    def arrive(pair):
        for g in (2 * pair, 2 * pair + 1):
            for copy in copies[g]:
                copy.wait()

    def activation(g):
        for c in range(4 * g, 4 * g + 4):
            for x in range(4):
                dz_ref[c, x] = gelu_backward(
                    pre_ref[c, x].astype(f32), cot_ref[c, x].astype(f32)
                ).astype(bf16)

    def along_time(field, g):
        ref = (dz_ref, inp_ref)[field]
        rows = jnp.concatenate([ref[4 * g + c].reshape(512, 128) for c in range(4)], axis=1)
        sect = jnp.dot(rows, time_ref[...], preferred_element_type=f32).astype(bf16)
        side = g % 2
        for x in range(4):
            for q in range(2):
                sect_ref[
                    field,
                    256 * x + 128 * q : 256 * x + 128 * q + 128,
                    128 * side : 128 * side + 128,
                ] = sect[128 * x : 128 * x + 128, 128 * q : 128 * q + 128]

    def along_y(field):
        spectra = jnp.dot(table_ref[...], sect_ref[field], preferred_element_type=f32)
        first, second = spectra[:, :128], spectra[:, 128:]
        return (
            jnp.where(low, first, pltpu.roll(second, 64, 1)).reshape(64, 8, 128),
            jnp.where(low, pltpu.roll(first, 64, 1), second).reshape(64, 8, 128),
        )

    def hold(halves):
        for h in range(2):
            half_ref[h] = halves[h]

    def send(pair, halves):
        for h in range(2):
            both = jnp.concatenate([halves[h], half_ref[h]], axis=1)
            send_ref[:, h, :, 128 * pair : 128 * pair + 128] = both.astype(bf16)
        lanes = (slice(None), slice(None), slice(None), pl.ds(128 * pair, 128))
        copy = pltpu.make_async_copy(send_ref.at[lanes], send_hbm.at[lanes], sent.at[pair])
        copy.start()
        return copy

    arrive(0)
    along_time(1, 0)
    activation(0)
    along_time(1, 1)
    activation(1)
    hold(along_y(1))
    arrive(1)
    along_time(0, 0)
    along_time(0, 1)
    activation(2)
    first = send(0, along_y(0))
    along_time(1, 2)
    along_time(1, 3)
    activation(3)
    hold(along_y(1))
    along_time(0, 2)
    along_time(0, 3)
    second = send(1, along_y(0))
    first.wait()
    second.wait()


def middle_kernel(scale_in, scale_out):
    def kernel(
        core_ref,
        recv_ref,
        w_hbm,
        xi_ref,
        send_hbm,
        mine_ref,
        other_ref,
        w_ref,
        back_ref,
        g_ref,
        gr_ref,
        send_ref,
        loaded,
        sent,
    ):
        loads = [
            pltpu.make_async_copy(w_hbm.at[pl.ds(8 * n, 8)], w_ref.at[pl.ds(8 * n, 8)], loaded.at[n])
            for n in range(2)
        ]
        for load in loads:
            load.start()
        core = core_ref[0]
        line = xi_ref[...].T
        block = recv_ref[...].astype(f32)
        hats = []
        for f, scale in enumerate((scale_out, scale_in)):
            rows = block[:, 8 * f : 8 * f + 8, :].reshape(1024, 256).astype(bf16)
            summed = jnp.dot(line, rows, preferred_element_type=f32)
            hats.append((scale * summed).T.astype(bf16).astype(f32))
        grad = hats[0]
        g_ref[0] = grad
        g_ref[1] = hats[1]
        gr_ref[...] = pltpu.roll(grad, 64, 1)
        for f in range(2):
            for c in range(16):
                mine_ref[f, c] = g_ref[f, pl.ds(16 * c + 8 * core, 8), :].astype(bf16)
                other_ref[f, c] = g_ref[f, pl.ds(16 * c + 8 - 8 * core, 8), :].astype(bf16)
        low = low_lanes((16, 128))
        for i in range(16):
            if i % 8 == 0:
                loads[i // 8].wait()
            same = jnp.zeros((16, 128), f32)
            cross = jnp.zeros((16, 128), f32)
            for o in range(16):
                weight = w_ref[i, o].astype(f32)
                same = same + weight * g_ref[0, 16 * o : 16 * o + 16, :]
                cross = cross + weight * gr_ref[16 * o : 16 * o + 16, :]
            back = jnp.where(low, same + pltpu.roll(same, 64, 1), pltpu.roll(cross, 64, 1) - cross)
            back_ref[16 * i : 16 * i + 16, :] = back.astype(bf16)
        copies = []
        for part in range(2):
            grid_rows = lax.dot_general(
                xi_ref[512 * part : 512 * part + 512],
                back_ref[...],
                (((1,), (1,)), ((), ())),
                preferred_element_type=f32,
            )
            block = pl.ds(64 * part, 64)
            send_ref[block] = grid_rows.reshape(64, 8, 256).astype(bf16)
            copies.append(
                pltpu.make_async_copy(send_ref.at[block], send_hbm.at[block], sent.at[part])
            )
            copies[-1].start()
        for copy in copies:
            copy.wait()

    return kernel


def mode_kernel(mine_ref, other_ref, out_ref, g_ref, gx_ref):
    low = low_lanes((16, 8, 128))
    for s, ref in enumerate((mine_ref, other_ref)):
        grad = ref[0].astype(f32)
        rolled = pltpu.roll(grad, 64, 2)
        g_ref[s] = grad
        gx_ref[s] = jnp.where(low, rolled, -rolled)
    low = low_lanes((8, 128))
    for i in range(16):
        real, imag = [], []
        for ref in (mine_ref, other_ref):
            value = ref[1, i].astype(f32)
            rolled = pltpu.roll(value, 64, 1)
            real.append(jnp.where(low, value, rolled))
            imag.append(jnp.where(low, rolled, value))
        for o in range(16):
            out_ref[i, o] = (
                real[0] * g_ref[0, o]
                + imag[0] * gx_ref[0, o]
                + (real[1] * g_ref[1, o] + imag[1] * gx_ref[1, o])
            )


def bypass_kernel(
    b_ref, dz_ref, xi_hbm, out_hbm, xi_ref, out_ref, sems, sent
):
    copies = [
        pltpu.make_async_copy(src, dst, sems.at[n])
        for n, (src, dst) in enumerate(((xi_hbm, xi_ref),))
    ]
    for copy in copies:
        copy.start()
    row = lax.broadcasted_iota(jnp.int32, (256, 16), 0)
    col = lax.broadcasted_iota(jnp.int32, (256, 16), 1)
    spread = jnp.where(row // 16 == col, 1.0, 0.0).astype(bf16)
    left = jnp.dot(spread, b_ref[...], preferred_element_type=f32).astype(bf16)
    full = lax.dot_general(left, spread, (((1,), (1,)), ((), ())), preferred_element_type=f32)
    row = lax.broadcasted_iota(jnp.int32, (256, 256), 0)
    col = lax.broadcasted_iota(jnp.int32, (256, 256), 1)
    mix = jnp.where(row % 16 == col % 16, full, 0.0).astype(bf16)
    def cell(x, carry):
        rows = jnp.concatenate(
            [
                jnp.concatenate([dz_ref[o, x, 16 * b : 16 * b + 16, :] for o in range(16)], axis=0)
                for b in range(8)
            ],
            axis=1,
        )
        mixed = jnp.dot(mix, rows, preferred_element_type=f32)
        for i in range(16):
            for b in range(8):
                out_ref[i, x, 16 * b : 16 * b + 16, :] = mixed[
                    16 * i : 16 * i + 16, 128 * b : 128 * b + 128
                ]
        return carry

    lax.fori_loop(0, 4, cell, 0)
    copies.append(pltpu.make_async_copy(out_ref, out_hbm, sent))
    copies[-1].start()
    for copy in copies:
        copy.wait()


def inverse_kernel(scale_in):
    def kernel(recv_ref, plane_ref, time_ref, bypass_hbm, out_hbm, rows_ref, bypass_ref, out_ref, loads, sems):
        arriving = [
            pltpu.make_async_copy(bypass_hbm.at[:, x], bypass_ref.at[:, x], loads.at[x])
            for x in range(4)
        ]
        for copy in arriving:
            copy.start()
        block = recv_ref[...].astype(f32).reshape(64, 2, 8, 256)
        low = low_lanes((512, 128))
        for v in range(2):
            first = block[:, 0, :, 128 * v : 128 * v + 128].reshape(512, 128)
            second = block[:, 1, :, 128 * v : 128 * v + 128].reshape(512, 128)
            rows_ref[2 * v] = jnp.where(low, first, pltpu.roll(second, 64, 1))
            rows_ref[2 * v + 1] = jnp.where(low, pltpu.roll(first, 64, 1), second)
        copies = []
        for x in range(4):
            spectra = jnp.concatenate(
                [
                    jnp.concatenate(
                        [rows_ref[g, pl.ds(2 * x + a, 64, stride=8), :] for a in range(2)], axis=0
                    )
                    for g in range(4)
                ],
                axis=1,
            ).astype(bf16)
            joined = jnp.dot(plane_ref[...], spectra, preferred_element_type=f32).astype(bf16)
            stacked = jnp.concatenate(
                [
                    jnp.concatenate(
                        [
                            joined[128 * q : 128 * q + 128, 128 * g : 128 * g + 128]
                            for q in range(2)
                        ],
                        axis=1,
                    )
                    for g in range(4)
                ],
                axis=0,
            )
            arriving[x].wait()
            spectral = jnp.dot(stacked, time_ref[...], preferred_element_type=f32)
            for g in range(4):
                for c in range(4):
                    out_ref[4 * g + c, x] = (
                        scale_in * spectral[128 * g : 128 * g + 128, 128 * c : 128 * c + 128]
                        + bypass_ref[4 * g + c, x]
                    ).astype(bf16)
            copies.append(
                pltpu.make_async_copy(out_ref.at[:, x], out_hbm.at[:, x], sems.at[x])
            )
            copies[-1].start()
        for copy in copies:
            copy.wait()

    return kernel


def remote(array):
    return pltpu.with_memory_space_constraint(array, pltpu.HBM)


def local(array):
    return pltpu.with_memory_space_constraint(array, pltpu.VMEM)


def shards(inputs, preact, cotangent, mode_weight, bypass_weight):
    slab = inputs.shape[2]
    cells_y = inputs.shape[3]
    cells_time = inputs.shape[4]
    cells_x = slab * lax.axis_size("gx")
    modes_x = mode_weight.shape[3] // 2
    cell_count = cells_x * cells_y * cells_time
    scale_in = float(modes_x * MY * MT * cell_count) ** (-0.25)
    scale_out = float(cell_count) ** (-0.5)
    time_forward, time_inverse, plane, plane_back, line = constants(
        cells_x, cells_y, cells_time, modes_x, slab
    )
    core = lax.axis_index("sa").astype(jnp.int32).reshape(1)

    vmem = pl.BlockSpec(memory_space=pltpu.VMEM)
    hbm = pl.BlockSpec(memory_space=pltpu.HBM)
    field = (16, 4, 128, 128)
    send, dz = pl.pallas_call(
        forward_kernel,
        in_specs=[hbm] * 5,
        out_specs=[hbm, vmem],
        out_shape=[pltpu.HBM((64, 2, 16, 256), bf16), pltpu.VMEM(field, bf16)],
        scratch_shapes=[pltpu.VMEM(field, bf16)] * 3
        + [
            pltpu.VMEM(time_forward.shape, bf16),
            pltpu.VMEM(plane.shape, bf16),
            pltpu.VMEM((64, 2, 16, 256), bf16),
            pltpu.VMEM((512, 1024), bf16),
            pltpu.VMEM((2, 1024, 256), bf16),
            pltpu.VMEM((2, 64, 8, 128), f32),
            pltpu.SemaphoreType.DMA((3, 4)),
            pltpu.SemaphoreType.DMA((2,)),
            pltpu.SemaphoreType.DMA((2,)),
        ],
        name="forward",
        compiler_params=pltpu.CompilerParams(vmem_limit_bytes=24 << 20),
    )(
        remote(preact[0]),
        remote(cotangent[0]),
        remote(inputs[0]),
        remote(time_forward),
        remote(plane),
    )
    recv = lax.all_to_all(
        send.reshape(128, 16, 256), "gx", split_axis=0, concat_axis=0, tiled=True
    )
    bypass, line = pl.pallas_call(
        bypass_kernel,
        in_specs=[vmem, vmem, hbm],
        out_specs=[hbm, vmem],
        out_shape=[
            pltpu.HBM(field, f32),
            pltpu.VMEM(line.shape, bf16),
        ],
        scratch_shapes=[
            pltpu.VMEM(field, f32),
            pltpu.SemaphoreType.DMA((1,)),
            pltpu.SemaphoreType.DMA,
        ],
        name="bypass",
        compiler_params=pltpu.CompilerParams(vmem_limit_bytes=24 << 20),
    )(bypass_weight, local(dz), remote(line))
    rows, mine, other = pl.pallas_call(
        middle_kernel(scale_in, scale_out),
        in_specs=[pl.BlockSpec(memory_space=pltpu.SMEM), vmem, hbm, vmem],
        out_specs=[hbm, vmem, vmem],
        out_shape=[
            pltpu.HBM((128, 8, 256), bf16),
            pltpu.VMEM((2, 16, 8, 128), bf16),
            jax.ShapeDtypeStruct((2, 16, 8, 128), bf16),
        ],
        scratch_shapes=[
            pltpu.VMEM(mode_weight.shape, bf16),
            pltpu.VMEM((256, 128), bf16),
            pltpu.VMEM((2, 256, 128), f32),
            pltpu.VMEM((256, 128), f32),
            pltpu.VMEM((128, 8, 256), bf16),
            pltpu.SemaphoreType.DMA((2,)),
            pltpu.SemaphoreType.DMA((2,)),
        ],
        name="middle",
        compiler_params=pltpu.CompilerParams(vmem_limit_bytes=24 << 20),
    )(core, local(recv), remote(mode_weight), local(line))
    back = lax.all_to_all(rows, "gx", split_axis=0, concat_axis=0, tiled=True)
    theirs = lax.ppermute(other, "sa", [(0, 1), (1, 0)])
    mode_grad = pl.pallas_call(
        mode_kernel,
        in_specs=[vmem, vmem],
        out_specs=vmem,
        out_shape=jax.ShapeDtypeStruct((16, 16, 8, 128), f32),
        scratch_shapes=[pltpu.VMEM((2, 16, 8, 128), f32), pltpu.VMEM((2, 16, 8, 128), f32)],
        name="modes",
        compiler_params=pltpu.CompilerParams(vmem_limit_bytes=24 << 20),
    )(local(mine), local(theirs))
    input_grad = pl.pallas_call(
        inverse_kernel(scale_in),
        in_specs=[vmem, vmem, vmem, hbm],
        out_specs=hbm,
        out_shape=jax.ShapeDtypeStruct(field, bf16),
        scratch_shapes=[
            pltpu.VMEM((4, 512, 128), f32),
            pltpu.VMEM(field, f32),
            pltpu.VMEM(field, bf16),
            pltpu.SemaphoreType.DMA((4,)),
            pltpu.SemaphoreType.DMA((4,)),
        ],
        name="inverse",
        compiler_params=pltpu.CompilerParams(vmem_limit_bytes=24 << 20),
    )(local(back), local(plane_back), local(time_inverse), remote(bypass))
    return (input_grad[None], mode_grad)


def solution(mesh):
    field = P("sa", None, "gx", None, None)
    return jax.shard_map(
        shards,
        mesh=mesh,
        in_specs=(field, field, field, P(None, None, "gx", None), P()),
        out_specs=(field, P(None, None, ("gx", "sa"), None)),
        check_vma=False,
    )
```

```python
import math

import jax
import jax.numpy as jnp
import numpy as np
from jax import lax
from jax.experimental import pallas as pl
from jax.experimental.pallas import tpu as pltpu
from jax.sharding import PartitionSpec as P

MY = 64
MT = 32

root_half = math.sqrt(0.5)
gauss_norm = 1.0 / math.sqrt(2.0 * math.pi)
f32 = jnp.float32
bf16 = jnp.bfloat16


def tables(kept_count, length, two_sided):
    frequency = np.arange(kept_count)
    if two_sided:
        frequency = np.where(
            frequency < kept_count // 2, frequency, frequency + (length - kept_count)
        )
    product = frequency[:, None] * np.arange(length)[None, :] % length
    phase_angle = product * (2.0 * math.pi / length)
    return (
        np.cos(phase_angle).astype(np.float32).astype(bf16).astype(np.float32),
        np.sin(phase_angle).astype(np.float32).astype(bf16).astype(np.float32),
    )


def constants(cells_x, cells_y, cells_time, modes_x, slab):
    ct, st = tables(MT, cells_time, False)
    cy, sy = tables(MY, cells_y, True)
    cx, sx = tables(modes_x, cells_x, True)
    four = np.eye(4, dtype=np.float32)
    time = np.stack([ct, -st]).reshape(2, 2, MT // 2, cells_time)
    time_forward = np.einsum("cd,qhkt->ctqhdk", four, time).reshape(4 * cells_time, -1)
    time_inverse = np.einsum("cd,qhkt->qhckdt", four, time).reshape(-1, 4 * cells_time)
    plane = np.block([[cy, sy], [-sy, cy]])
    plane_rows = plane.reshape(2, MY, 1, -1).repeat(slab, 2).transpose(1, 2, 0, 3)
    plane_rows = plane_rows.reshape(MY * slab * 2, -1)
    line = np.stack([np.concatenate([cx, -sx]), np.concatenate([sx, cx])], -1)
    line = line.reshape(2 * modes_x, -1).T
    return [
        a.astype(bf16) for a in (time_forward, time_inverse, plane_rows, plane.T, line)
    ]


def low_lanes(shape):
    return lax.broadcasted_iota(jnp.int32, shape, len(shape) - 1) < 64


def gelu_backward(values, cotangent):
    scaled = values * root_half
    density = jnp.exp2((scaled * scaled) * -math.log2(math.e))
    slope = (1.0 + lax.erf(scaled)) + (scaled * (4.0 * root_half * gauss_norm)) * density
    return (cotangent * 0.5) * slope


def forward_kernel(
    pre_hbm,
    cot_hbm,
    inp_hbm,
    time_hbm,
    plane_hbm,
    send_hbm,
    dz_ref,
    pre_ref,
    cot_ref,
    inp_ref,
    time_ref,
    plane_ref,
    send_ref,
    table_ref,
    sect_ref,
    half_ref,
    sems,
    table_sems,
    sent,
):
    plane_copy = pltpu.make_async_copy(plane_hbm, plane_ref, table_sems.at[0])
    time_copy = pltpu.make_async_copy(time_hbm, time_ref, table_sems.at[1])
    plane_copy.start()
    time_copy.start()
    copies = []
    for g in range(4):
        part = pl.ds(4 * g, 4)
        trio = [
            pltpu.make_async_copy(src.at[part], dst.at[part], sems.at[n, g])
            for n, (src, dst) in enumerate(
                ((inp_hbm, inp_ref), (pre_hbm, pre_ref), (cot_hbm, cot_ref))
            )
        ]
        for copy in trio:
            copy.start()
        copies.append(trio)
    row_x = lax.broadcasted_iota(jnp.int32, (512, 256), 0) // 2 % 4
    plane_copy.wait()
    plane = plane_ref[...].astype(f32)
    for x in range(4):
        table_ref[:, 256 * x : 256 * x + 256] = jnp.where(row_x == x, plane, 0.0).astype(bf16)
    low = low_lanes((512, 128))
    time_copy.wait()

    def arrive(g):
        for copy in copies[g]:
            copy.wait()

    def activation(g):
        for c in range(4 * g, 4 * g + 4):
            for x in range(4):
                dz_ref[c, x] = gelu_backward(
                    pre_ref[c, x].astype(f32), cot_ref[c, x].astype(f32)
                ).astype(bf16)

    def along_time(field, g):
        ref = (dz_ref, inp_ref)[field]
        rows = jnp.concatenate([ref[4 * g + c].reshape(512, 128) for c in range(4)], axis=1)
        sect = jnp.dot(rows, time_ref[...], preferred_element_type=f32).astype(bf16)
        side = g % 2
        for x in range(4):
            for q in range(2):
                sect_ref[
                    field,
                    256 * x + 128 * q : 256 * x + 128 * q + 128,
                    128 * side : 128 * side + 128,
                ] = sect[128 * x : 128 * x + 128, 128 * q : 128 * q + 128]

    def along_y(field):
        spectra = jnp.dot(table_ref[...], sect_ref[field], preferred_element_type=f32)
        first, second = spectra[:, :128], spectra[:, 128:]
        return (
            jnp.where(low, first, pltpu.roll(second, 64, 1)).reshape(64, 8, 128),
            jnp.where(low, pltpu.roll(first, 64, 1), second).reshape(64, 8, 128),
        )

    def hold(halves):
        for h in range(2):
            half_ref[h] = halves[h]

    def send(pair, halves):
        for h in range(2):
            both = jnp.concatenate([halves[h], half_ref[h]], axis=1)
            send_ref[:, h, :, 128 * pair : 128 * pair + 128] = both.astype(bf16)
        lanes = (slice(None), slice(None), slice(None), pl.ds(128 * pair, 128))
        copy = pltpu.make_async_copy(send_ref.at[lanes], send_hbm.at[lanes], sent.at[pair])
        copy.start()
        return copy

    arrive(0)
    along_time(1, 0)
    activation(0)
    arrive(1)
    along_time(1, 1)
    along_time(0, 0)
    activation(1)
    hold(along_y(1))
    arrive(2)
    along_time(0, 1)
    activation(2)
    first = send(0, along_y(0))
    along_time(1, 2)
    arrive(3)
    along_time(1, 3)
    along_time(0, 2)
    activation(3)
    hold(along_y(1))
    along_time(0, 3)
    second = send(1, along_y(0))
    first.wait()
    second.wait()


def middle_kernel(scale_in, scale_out):
    def kernel(
        core_ref,
        recv_ref,
        w_ref,
        xi_ref,
        send_hbm,
        mine_ref,
        other_ref,
        back_ref,
        g_ref,
        gr_ref,
        send_ref,
        sent,
    ):
        core = core_ref[0]
        line = xi_ref[...].T
        block = recv_ref[...].astype(f32)
        hats = []
        for f, scale in enumerate((scale_out, scale_in)):
            rows = block[:, 8 * f : 8 * f + 8, :].reshape(1024, 256).astype(bf16)
            summed = jnp.dot(line, rows, preferred_element_type=f32)
            hats.append((scale * summed).T.astype(bf16).astype(f32))
        grad = hats[0]
        g_ref[0] = grad
        g_ref[1] = hats[1]
        gr_ref[...] = pltpu.roll(grad, 64, 1)
        for f in range(2):
            for c in range(16):
                mine_ref[f, c] = g_ref[f, pl.ds(16 * c + 8 * core, 8), :].astype(bf16)
                other_ref[f, c] = g_ref[f, pl.ds(16 * c + 8 - 8 * core, 8), :].astype(bf16)
        low = low_lanes((16, 128))
        for i in range(16):
            same = jnp.zeros((16, 128), f32)
            cross = jnp.zeros((16, 128), f32)
            for o in range(16):
                weight = w_ref[i, o].astype(f32)
                same = same + weight * g_ref[0, 16 * o : 16 * o + 16, :]
                cross = cross + weight * gr_ref[16 * o : 16 * o + 16, :]
            back = jnp.where(low, same + pltpu.roll(same, 64, 1), pltpu.roll(cross, 64, 1) - cross)
            back_ref[16 * i : 16 * i + 16, :] = back.astype(bf16)
        copies = []
        for part in range(2):
            grid_rows = lax.dot_general(
                xi_ref[512 * part : 512 * part + 512],
                back_ref[...],
                (((1,), (1,)), ((), ())),
                preferred_element_type=f32,
            )
            block = pl.ds(64 * part, 64)
            send_ref[block] = grid_rows.reshape(64, 8, 256).astype(bf16)
            copies.append(
                pltpu.make_async_copy(send_ref.at[block], send_hbm.at[block], sent.at[part])
            )
            copies[-1].start()
        for copy in copies:
            copy.wait()

    return kernel


def mode_kernel(mine_ref, other_ref, out_ref, g_ref, gx_ref):
    low = low_lanes((16, 8, 128))
    for s, ref in enumerate((mine_ref, other_ref)):
        grad = ref[0].astype(f32)
        rolled = pltpu.roll(grad, 64, 2)
        g_ref[s] = grad
        gx_ref[s] = jnp.where(low, rolled, -rolled)
    low = low_lanes((8, 128))
    for i in range(16):
        real, imag = [], []
        for ref in (mine_ref, other_ref):
            value = ref[1, i].astype(f32)
            rolled = pltpu.roll(value, 64, 1)
            real.append(jnp.where(low, value, rolled))
            imag.append(jnp.where(low, rolled, value))
        for o in range(16):
            out_ref[i, o] = (
                real[0] * g_ref[0, o]
                + imag[0] * gx_ref[0, o]
                + (real[1] * g_ref[1, o] + imag[1] * gx_ref[1, o])
            )


def bypass_kernel(
    b_ref, dz_ref, xi_hbm, out_hbm, xi_ref, out_ref, sems, sent
):
    copies = [
        pltpu.make_async_copy(src, dst, sems.at[n])
        for n, (src, dst) in enumerate(((xi_hbm, xi_ref),))
    ]
    for copy in copies:
        copy.start()
    row = lax.broadcasted_iota(jnp.int32, (256, 16), 0)
    col = lax.broadcasted_iota(jnp.int32, (256, 16), 1)
    spread = jnp.where(row // 16 == col, 1.0, 0.0).astype(bf16)
    left = jnp.dot(spread, b_ref[...], preferred_element_type=f32).astype(bf16)
    full = lax.dot_general(left, spread, (((1,), (1,)), ((), ())), preferred_element_type=f32)
    row = lax.broadcasted_iota(jnp.int32, (256, 256), 0)
    col = lax.broadcasted_iota(jnp.int32, (256, 256), 1)
    mix = jnp.where(row % 16 == col % 16, full, 0.0).astype(bf16)
    def cell(x, carry):
        rows = jnp.concatenate(
            [
                jnp.concatenate([dz_ref[o, x, 16 * b : 16 * b + 16, :] for o in range(16)], axis=0)
                for b in range(8)
            ],
            axis=1,
        )
        mixed = jnp.dot(mix, rows, preferred_element_type=f32)
        for i in range(16):
            for b in range(8):
                out_ref[i, x, 16 * b : 16 * b + 16, :] = mixed[
                    16 * i : 16 * i + 16, 128 * b : 128 * b + 128
                ]
        return carry

    lax.fori_loop(0, 4, cell, 0)
    copies.append(pltpu.make_async_copy(out_ref, out_hbm, sent))
    copies[-1].start()
    for copy in copies:
        copy.wait()


def fetch_kernel(w_hbm, after_ref, w_ref, sem):
    copy = pltpu.make_async_copy(w_hbm, w_ref, sem)
    copy.start()
    copy.wait()


def inverse_kernel(scale_in):
    def kernel(recv_ref, plane_ref, time_ref, bypass_hbm, out_hbm, rows_ref, bypass_ref, out_ref, loads, sems):
        arriving = [
            pltpu.make_async_copy(bypass_hbm.at[:, x], bypass_ref.at[:, x], loads.at[x])
            for x in range(4)
        ]
        for copy in arriving:
            copy.start()
        block = recv_ref[...].astype(f32).reshape(64, 2, 8, 256)
        low = low_lanes((512, 128))
        for v in range(2):
            first = block[:, 0, :, 128 * v : 128 * v + 128].reshape(512, 128)
            second = block[:, 1, :, 128 * v : 128 * v + 128].reshape(512, 128)
            rows_ref[2 * v] = jnp.where(low, first, pltpu.roll(second, 64, 1))
            rows_ref[2 * v + 1] = jnp.where(low, pltpu.roll(first, 64, 1), second)
        copies = []
        for x in range(4):
            spectra = jnp.concatenate(
                [
                    jnp.concatenate(
                        [rows_ref[g, pl.ds(2 * x + a, 64, stride=8), :] for a in range(2)], axis=0
                    )
                    for g in range(4)
                ],
                axis=1,
            ).astype(bf16)
            joined = jnp.dot(plane_ref[...], spectra, preferred_element_type=f32).astype(bf16)
            stacked = jnp.concatenate(
                [
                    jnp.concatenate(
                        [
                            joined[128 * q : 128 * q + 128, 128 * g : 128 * g + 128]
                            for q in range(2)
                        ],
                        axis=1,
                    )
                    for g in range(4)
                ],
                axis=0,
            )
            arriving[x].wait()
            spectral = jnp.dot(stacked, time_ref[...], preferred_element_type=f32)
            for g in range(4):
                for c in range(4):
                    out_ref[4 * g + c, x] = (
                        scale_in * spectral[128 * g : 128 * g + 128, 128 * c : 128 * c + 128]
                        + bypass_ref[4 * g + c, x]
                    ).astype(bf16)
            copies.append(
                pltpu.make_async_copy(out_ref.at[:, x], out_hbm.at[:, x], sems.at[x])
            )
            copies[-1].start()
        for copy in copies:
            copy.wait()

    return kernel


def remote(array):
    return pltpu.with_memory_space_constraint(array, pltpu.HBM)


def local(array):
    return pltpu.with_memory_space_constraint(array, pltpu.VMEM)


def shards(inputs, preact, cotangent, mode_weight, bypass_weight):
    slab = inputs.shape[2]
    cells_y = inputs.shape[3]
    cells_time = inputs.shape[4]
    cells_x = slab * lax.axis_size("gx")
    modes_x = mode_weight.shape[3] // 2
    cell_count = cells_x * cells_y * cells_time
    scale_in = float(modes_x * MY * MT * cell_count) ** (-0.25)
    scale_out = float(cell_count) ** (-0.5)
    time_forward, time_inverse, plane, plane_back, line = constants(
        cells_x, cells_y, cells_time, modes_x, slab
    )
    core = lax.axis_index("sa").astype(jnp.int32).reshape(1)

    vmem = pl.BlockSpec(memory_space=pltpu.VMEM)
    hbm = pl.BlockSpec(memory_space=pltpu.HBM)
    field = (16, 4, 128, 128)
    send, dz = pl.pallas_call(
        forward_kernel,
        in_specs=[hbm] * 5,
        out_specs=[hbm, vmem],
        out_shape=[pltpu.HBM((64, 2, 16, 256), bf16), pltpu.VMEM(field, bf16)],
        scratch_shapes=[pltpu.VMEM(field, bf16)] * 3
        + [
            pltpu.VMEM(time_forward.shape, bf16),
            pltpu.VMEM(plane.shape, bf16),
            pltpu.VMEM((64, 2, 16, 256), bf16),
            pltpu.VMEM((512, 1024), bf16),
            pltpu.VMEM((2, 1024, 256), bf16),
            pltpu.VMEM((2, 64, 8, 128), f32),
            pltpu.SemaphoreType.DMA((3, 4)),
            pltpu.SemaphoreType.DMA((2,)),
            pltpu.SemaphoreType.DMA((2,)),
        ],
        name="forward",
        compiler_params=pltpu.CompilerParams(vmem_limit_bytes=24 << 20),
    )(
        remote(preact[0]),
        remote(cotangent[0]),
        remote(inputs[0]),
        remote(time_forward),
        remote(plane),
    )
    recv = lax.all_to_all(
        send.reshape(128, 16, 256), "gx", split_axis=0, concat_axis=0, tiled=True
    )
    bypass, line = pl.pallas_call(
        bypass_kernel,
        in_specs=[vmem, vmem, hbm],
        out_specs=[hbm, vmem],
        out_shape=[
            pltpu.HBM(field, f32),
            pltpu.VMEM(line.shape, bf16),
        ],
        scratch_shapes=[
            pltpu.VMEM(field, f32),
            pltpu.SemaphoreType.DMA((1,)),
            pltpu.SemaphoreType.DMA,
        ],
        name="bypass",
        compiler_params=pltpu.CompilerParams(vmem_limit_bytes=24 << 20),
    )(bypass_weight, local(dz), remote(line))
    weights = pl.pallas_call(
        fetch_kernel,
        in_specs=[hbm, vmem],
        out_specs=vmem,
        out_shape=pltpu.VMEM(mode_weight.shape, bf16),
        scratch_shapes=[pltpu.SemaphoreType.DMA],
        name="fetch",
        compiler_params=pltpu.CompilerParams(vmem_limit_bytes=24 << 20),
    )(remote(mode_weight), local(line))
    rows, mine, other = pl.pallas_call(
        middle_kernel(scale_in, scale_out),
        in_specs=[pl.BlockSpec(memory_space=pltpu.SMEM), vmem, vmem, vmem],
        out_specs=[hbm, vmem, vmem],
        out_shape=[
            pltpu.HBM((128, 8, 256), bf16),
            pltpu.VMEM((2, 16, 8, 128), bf16),
            jax.ShapeDtypeStruct((2, 16, 8, 128), bf16),
        ],
        scratch_shapes=[
            pltpu.VMEM((256, 128), bf16),
            pltpu.VMEM((2, 256, 128), f32),
            pltpu.VMEM((256, 128), f32),
            pltpu.VMEM((128, 8, 256), bf16),
            pltpu.SemaphoreType.DMA((2,)),
        ],
        name="middle",
        compiler_params=pltpu.CompilerParams(vmem_limit_bytes=24 << 20),
    )(core, local(recv), local(weights), local(line))
    back = lax.all_to_all(rows, "gx", split_axis=0, concat_axis=0, tiled=True)
    theirs = lax.ppermute(other, "sa", [(0, 1), (1, 0)])
    mode_grad = pl.pallas_call(
        mode_kernel,
        in_specs=[vmem, vmem],
        out_specs=vmem,
        out_shape=jax.ShapeDtypeStruct((16, 16, 8, 128), f32),
        scratch_shapes=[pltpu.VMEM((2, 16, 8, 128), f32), pltpu.VMEM((2, 16, 8, 128), f32)],
        name="modes",
        compiler_params=pltpu.CompilerParams(vmem_limit_bytes=24 << 20),
    )(local(mine), local(theirs))
    input_grad = pl.pallas_call(
        inverse_kernel(scale_in),
        in_specs=[vmem, vmem, vmem, hbm],
        out_specs=hbm,
        out_shape=jax.ShapeDtypeStruct(field, bf16),
        scratch_shapes=[
            pltpu.VMEM((4, 512, 128), f32),
            pltpu.VMEM(field, f32),
            pltpu.VMEM(field, bf16),
            pltpu.SemaphoreType.DMA((4,)),
            pltpu.SemaphoreType.DMA((4,)),
        ],
        name="inverse",
        compiler_params=pltpu.CompilerParams(vmem_limit_bytes=24 << 20),
    )(local(back), local(plane_back), local(time_inverse), remote(bypass))
    return (input_grad[None], mode_grad)


def solution(mesh):
    field = P("sa", None, "gx", None, None)
    return jax.shard_map(
        shards,
        mesh=mesh,
        in_specs=(field, field, field, P(None, None, "gx", None), P()),
        out_specs=(field, P(None, None, ("gx", "sa"), None)),
        check_vma=False,
    )
```

```python
import math

import jax
import jax.numpy as jnp
import numpy as np
from jax import lax
from jax.experimental import pallas as pl
from jax.experimental.pallas import tpu as pltpu
from jax.sharding import PartitionSpec as P

MY = 64
MT = 32

root_half = math.sqrt(0.5)
gauss_norm = 1.0 / math.sqrt(2.0 * math.pi)
f32 = jnp.float32
bf16 = jnp.bfloat16


def tables(kept_count, length, two_sided):
    frequency = np.arange(kept_count)
    if two_sided:
        frequency = np.where(
            frequency < kept_count // 2, frequency, frequency + (length - kept_count)
        )
    product = frequency[:, None] * np.arange(length)[None, :] % length
    phase_angle = product * (2.0 * math.pi / length)
    return (
        np.cos(phase_angle).astype(np.float32).astype(bf16).astype(np.float32),
        np.sin(phase_angle).astype(np.float32).astype(bf16).astype(np.float32),
    )


def constants(cells_x, cells_y, cells_time, modes_x, slab):
    ct, st = tables(MT, cells_time, False)
    cy, sy = tables(MY, cells_y, True)
    cx, sx = tables(modes_x, cells_x, True)
    four = np.eye(4, dtype=np.float32)
    time = np.stack([ct, -st]).reshape(2, 2, MT // 2, cells_time)
    time_forward = np.einsum("cd,qhkt->ctqhdk", four, time).reshape(4 * cells_time, -1)
    time_inverse = np.einsum("cd,qhkt->qhckdt", four, time).reshape(-1, 4 * cells_time)
    plane = np.block([[cy, sy], [-sy, cy]])
    plane_rows = plane.reshape(2, MY, 1, -1).repeat(2, 2).transpose(1, 2, 0, 3)
    plane_rows = plane_rows.reshape(MY * 4, -1)
    line = np.stack([np.concatenate([cx, -sx]), np.concatenate([sx, cx])], -1)
    line = line.reshape(2 * modes_x, -1).T
    return [
        a.astype(bf16) for a in (time_forward, time_inverse, plane_rows, plane.T, line)
    ]


def low_lanes(shape):
    return lax.broadcasted_iota(jnp.int32, shape, len(shape) - 1) < 64


def gelu_backward(values, cotangent):
    scaled = values * root_half
    density = jnp.exp2((scaled * scaled) * -math.log2(math.e))
    slope = (1.0 + lax.erf(scaled)) + (scaled * (4.0 * root_half * gauss_norm)) * density
    return (cotangent * 0.5) * slope


def forward_kernel(
    pre_hbm,
    cot_hbm,
    inp_hbm,
    time_hbm,
    plane_hbm,
    send_hbm,
    dz_ref,
    pre_ref,
    cot_ref,
    inp_ref,
    time_ref,
    plane_ref,
    send_ref,
    table_ref,
    sect_ref,
    half_ref,
    sems,
    table_sems,
    sent,
):
    plane_copy = pltpu.make_async_copy(plane_hbm, plane_ref, table_sems.at[0])
    time_copy = pltpu.make_async_copy(time_hbm, time_ref, table_sems.at[1])
    plane_copy.start()
    time_copy.start()
    copies = []
    for g in range(4):
        part = pl.ds(4 * g, 4)
        trio = [
            pltpu.make_async_copy(src.at[part], dst.at[part], sems.at[n, g])
            for n, (src, dst) in enumerate(
                ((inp_hbm, inp_ref), (pre_hbm, pre_ref), (cot_hbm, cot_ref))
            )
        ]
        for copy in trio:
            copy.start()
        copies.append(trio)
    row_x = lax.broadcasted_iota(jnp.int32, (256, 256), 0) // 2 % 2
    plane_copy.wait()
    plane = plane_ref[...].astype(f32)
    for x in range(2):
        table_ref[:, 256 * x : 256 * x + 256] = jnp.where(row_x == x, plane, 0.0).astype(bf16)
    top = lax.broadcasted_iota(jnp.int32, (32, 8, 128), 1) < 4
    low = low_lanes((256, 128))
    time_copy.wait()

    def arrive(g):
        for copy in copies[g]:
            copy.wait()

    def activation(g):
        for c in range(4 * g, 4 * g + 4):
            for x in range(4):
                dz_ref[c, x] = gelu_backward(
                    pre_ref[c, x].astype(f32), cot_ref[c, x].astype(f32)
                ).astype(bf16)

    def along_time(field, g):
        ref = (dz_ref, inp_ref)[field]
        rows = jnp.concatenate([ref[4 * g + c].reshape(512, 128) for c in range(4)], axis=1)
        sect = jnp.dot(rows, time_ref[...], preferred_element_type=f32).astype(bf16)
        side = g % 2
        for x in range(4):
            for q in range(2):
                sect_ref[
                    field,
                    256 * x + 128 * q : 256 * x + 128 * q + 128,
                    128 * side : 128 * side + 128,
                ] = sect[128 * x : 128 * x + 128, 128 * q : 128 * q + 128]

    def along_y(field):
        parts = []
        for pair in range(2):
            spectra = jnp.dot(
                table_ref[...],
                sect_ref[field, 512 * pair : 512 * pair + 512, :],
                preferred_element_type=f32,
            )
            first, second = spectra[:, :128], spectra[:, 128:]
            parts.append(
                (
                    jnp.where(low, first, pltpu.roll(second, 64, 1)).reshape(32, 8, 128),
                    jnp.where(low, pltpu.roll(first, 64, 1), second).reshape(32, 8, 128),
                )
            )
        halves = []
        for h in range(2):
            one, two = parts[0][h], parts[1][h]
            even = jnp.where(top, one, pltpu.roll(two, 4, 1))
            odd = jnp.where(top, pltpu.roll(one, 4, 1), two)
            halves.append(jnp.stack([even, odd], axis=1).reshape(64, 8, 128))
        return halves

    def hold(halves):
        for h in range(2):
            half_ref[h] = halves[h]

    def send(pair, halves):
        for h in range(2):
            both = jnp.concatenate([halves[h], half_ref[h]], axis=1)
            send_ref[:, h, :, 128 * pair : 128 * pair + 128] = both.astype(bf16)
        lanes = (slice(None), slice(None), slice(None), pl.ds(128 * pair, 128))
        copy = pltpu.make_async_copy(send_ref.at[lanes], send_hbm.at[lanes], sent.at[pair])
        copy.start()
        return copy

    for g in range(4):
        arrive(g)
    along_time(1, 0)
    activation(0)
    along_time(1, 1)
    along_time(0, 0)
    activation(1)
    hold(along_y(1))
    along_time(0, 1)
    activation(2)
    first = send(0, along_y(0))
    along_time(1, 2)
    along_time(1, 3)
    along_time(0, 2)
    activation(3)
    hold(along_y(1))
    along_time(0, 3)
    second = send(1, along_y(0))
    first.wait()
    second.wait()


def middle_kernel(scale_in, scale_out):
    def kernel(
        core_ref,
        recv_ref,
        w_ref,
        xi_ref,
        send_hbm,
        mine_ref,
        other_ref,
        back_ref,
        g_ref,
        gr_ref,
        send_ref,
        sent,
    ):
        core = core_ref[0]
        line = xi_ref[...].T
        block = recv_ref[...].astype(f32)
        hats = []
        for f, scale in enumerate((scale_out, scale_in)):
            rows = block[:, 8 * f : 8 * f + 8, :].reshape(1024, 256).astype(bf16)
            summed = jnp.dot(line, rows, preferred_element_type=f32)
            hats.append((scale * summed).T.astype(bf16).astype(f32))
        grad = hats[0]
        g_ref[0] = grad
        g_ref[1] = hats[1]
        gr_ref[...] = pltpu.roll(grad, 64, 1)
        for f in range(2):
            for c in range(16):
                mine_ref[f, c] = g_ref[f, pl.ds(16 * c + 8 * core, 8), :].astype(bf16)
                other_ref[f, c] = g_ref[f, pl.ds(16 * c + 8 - 8 * core, 8), :].astype(bf16)
        low = low_lanes((16, 128))
        for i in range(16):
            same = jnp.zeros((16, 128), f32)
            cross = jnp.zeros((16, 128), f32)
            for o in range(16):
                weight = w_ref[i, o].astype(f32)
                same = same + weight * g_ref[0, 16 * o : 16 * o + 16, :]
                cross = cross + weight * gr_ref[16 * o : 16 * o + 16, :]
            back = jnp.where(low, same + pltpu.roll(same, 64, 1), pltpu.roll(cross, 64, 1) - cross)
            back_ref[16 * i : 16 * i + 16, :] = back.astype(bf16)
        copies = []
        for part in range(2):
            grid_rows = lax.dot_general(
                xi_ref[512 * part : 512 * part + 512],
                back_ref[...],
                (((1,), (1,)), ((), ())),
                preferred_element_type=f32,
            )
            block = pl.ds(64 * part, 64)
            send_ref[block] = grid_rows.reshape(64, 8, 256).astype(bf16)
            copies.append(
                pltpu.make_async_copy(send_ref.at[block], send_hbm.at[block], sent.at[part])
            )
            copies[-1].start()
        for copy in copies:
            copy.wait()

    return kernel


def mode_kernel(mine_ref, other_ref, out_ref, g_ref, gx_ref):
    low = low_lanes((16, 8, 128))
    for s, ref in enumerate((mine_ref, other_ref)):
        grad = ref[0].astype(f32)
        rolled = pltpu.roll(grad, 64, 2)
        g_ref[s] = grad
        gx_ref[s] = jnp.where(low, rolled, -rolled)
    low = low_lanes((8, 128))
    for i in range(16):
        real, imag = [], []
        for ref in (mine_ref, other_ref):
            value = ref[1, i].astype(f32)
            rolled = pltpu.roll(value, 64, 1)
            real.append(jnp.where(low, value, rolled))
            imag.append(jnp.where(low, rolled, value))
        for o in range(16):
            out_ref[i, o] = (
                real[0] * g_ref[0, o]
                + imag[0] * gx_ref[0, o]
                + (real[1] * g_ref[1, o] + imag[1] * gx_ref[1, o])
            )


def bypass_kernel(
    b_ref, dz_ref, xi_hbm, out_hbm, xi_ref, out_ref, sems, sent
):
    copies = [
        pltpu.make_async_copy(src, dst, sems.at[n])
        for n, (src, dst) in enumerate(((xi_hbm, xi_ref),))
    ]
    for copy in copies:
        copy.start()
    row = lax.broadcasted_iota(jnp.int32, (256, 16), 0)
    col = lax.broadcasted_iota(jnp.int32, (256, 16), 1)
    spread = jnp.where(row // 16 == col, 1.0, 0.0).astype(bf16)
    left = jnp.dot(spread, b_ref[...], preferred_element_type=f32).astype(bf16)
    full = lax.dot_general(left, spread, (((1,), (1,)), ((), ())), preferred_element_type=f32)
    row = lax.broadcasted_iota(jnp.int32, (256, 256), 0)
    col = lax.broadcasted_iota(jnp.int32, (256, 256), 1)
    mix = jnp.where(row % 16 == col % 16, full, 0.0).astype(bf16)
    def cell(x, carry):
        rows = jnp.concatenate(
            [
                jnp.concatenate([dz_ref[o, x, 16 * b : 16 * b + 16, :] for o in range(16)], axis=0)
                for b in range(8)
            ],
            axis=1,
        )
        mixed = jnp.dot(mix, rows, preferred_element_type=f32)
        for i in range(16):
            for b in range(8):
                out_ref[i, x, 16 * b : 16 * b + 16, :] = mixed[
                    16 * i : 16 * i + 16, 128 * b : 128 * b + 128
                ]
        return carry

    lax.fori_loop(0, 4, cell, 0)
    copies.append(pltpu.make_async_copy(out_ref, out_hbm, sent))
    copies[-1].start()
    for copy in copies:
        copy.wait()


def fetch_kernel(w_hbm, after_ref, w_ref, sem):
    copy = pltpu.make_async_copy(w_hbm, w_ref, sem)
    copy.start()
    copy.wait()


def inverse_kernel(scale_in):
    def kernel(recv_ref, plane_ref, time_ref, bypass_hbm, out_hbm, rows_ref, bypass_ref, out_ref, loads, sems):
        arriving = [
            pltpu.make_async_copy(bypass_hbm.at[:, x], bypass_ref.at[:, x], loads.at[x])
            for x in range(4)
        ]
        for copy in arriving:
            copy.start()
        block = recv_ref[...].astype(f32).reshape(64, 2, 8, 256)
        low = low_lanes((512, 128))
        for v in range(2):
            first = block[:, 0, :, 128 * v : 128 * v + 128].reshape(512, 128)
            second = block[:, 1, :, 128 * v : 128 * v + 128].reshape(512, 128)
            rows_ref[2 * v] = jnp.where(low, first, pltpu.roll(second, 64, 1))
            rows_ref[2 * v + 1] = jnp.where(low, pltpu.roll(first, 64, 1), second)
        copies = []
        for x in range(4):
            spectra = jnp.concatenate(
                [
                    jnp.concatenate(
                        [rows_ref[g, pl.ds(2 * x + a, 64, stride=8), :] for a in range(2)], axis=0
                    )
                    for g in range(4)
                ],
                axis=1,
            ).astype(bf16)
            joined = jnp.dot(plane_ref[...], spectra, preferred_element_type=f32).astype(bf16)
            stacked = jnp.concatenate(
                [
                    jnp.concatenate(
                        [
                            joined[128 * q : 128 * q + 128, 128 * g : 128 * g + 128]
                            for q in range(2)
                        ],
                        axis=1,
                    )
                    for g in range(4)
                ],
                axis=0,
            )
            arriving[x].wait()
            spectral = jnp.dot(stacked, time_ref[...], preferred_element_type=f32)
            for g in range(4):
                for c in range(4):
                    out_ref[4 * g + c, x] = (
                        scale_in * spectral[128 * g : 128 * g + 128, 128 * c : 128 * c + 128]
                        + bypass_ref[4 * g + c, x]
                    ).astype(bf16)
            copies.append(
                pltpu.make_async_copy(out_ref.at[:, x], out_hbm.at[:, x], sems.at[x])
            )
            copies[-1].start()
        for copy in copies:
            copy.wait()

    return kernel


def remote(array):
    return pltpu.with_memory_space_constraint(array, pltpu.HBM)


def local(array):
    return pltpu.with_memory_space_constraint(array, pltpu.VMEM)


def shards(inputs, preact, cotangent, mode_weight, bypass_weight):
    slab = inputs.shape[2]
    cells_y = inputs.shape[3]
    cells_time = inputs.shape[4]
    cells_x = slab * lax.axis_size("gx")
    modes_x = mode_weight.shape[3] // 2
    cell_count = cells_x * cells_y * cells_time
    scale_in = float(modes_x * MY * MT * cell_count) ** (-0.25)
    scale_out = float(cell_count) ** (-0.5)
    time_forward, time_inverse, plane, plane_back, line = constants(
        cells_x, cells_y, cells_time, modes_x, slab
    )
    core = lax.axis_index("sa").astype(jnp.int32).reshape(1)

    vmem = pl.BlockSpec(memory_space=pltpu.VMEM)
    hbm = pl.BlockSpec(memory_space=pltpu.HBM)
    field = (16, 4, 128, 128)
    send, dz = pl.pallas_call(
        forward_kernel,
        in_specs=[hbm] * 5,
        out_specs=[hbm, vmem],
        out_shape=[pltpu.HBM((64, 2, 16, 256), bf16), pltpu.VMEM(field, bf16)],
        scratch_shapes=[pltpu.VMEM(field, bf16)] * 3
        + [
            pltpu.VMEM(time_forward.shape, bf16),
            pltpu.VMEM(plane.shape, bf16),
            pltpu.VMEM((64, 2, 16, 256), bf16),
            pltpu.VMEM((256, 512), bf16),
            pltpu.VMEM((2, 1024, 256), bf16),
            pltpu.VMEM((2, 64, 8, 128), f32),
            pltpu.SemaphoreType.DMA((3, 4)),
            pltpu.SemaphoreType.DMA((2,)),
            pltpu.SemaphoreType.DMA((2,)),
        ],
        name="forward",
        compiler_params=pltpu.CompilerParams(vmem_limit_bytes=24 << 20),
    )(
        remote(preact[0]),
        remote(cotangent[0]),
        remote(inputs[0]),
        remote(time_forward),
        remote(plane),
    )
    recv = lax.all_to_all(
        send.reshape(128, 16, 256), "gx", split_axis=0, concat_axis=0, tiled=True
    )
    bypass, line = pl.pallas_call(
        bypass_kernel,
        in_specs=[vmem, vmem, hbm],
        out_specs=[hbm, vmem],
        out_shape=[
            pltpu.HBM(field, f32),
            pltpu.VMEM(line.shape, bf16),
        ],
        scratch_shapes=[
            pltpu.VMEM(field, f32),
            pltpu.SemaphoreType.DMA((1,)),
            pltpu.SemaphoreType.DMA,
        ],
        name="bypass",
        compiler_params=pltpu.CompilerParams(vmem_limit_bytes=24 << 20),
    )(bypass_weight, local(dz), remote(line))
    weights = pl.pallas_call(
        fetch_kernel,
        in_specs=[hbm, vmem],
        out_specs=vmem,
        out_shape=pltpu.VMEM(mode_weight.shape, bf16),
        scratch_shapes=[pltpu.SemaphoreType.DMA],
        name="fetch",
        compiler_params=pltpu.CompilerParams(vmem_limit_bytes=24 << 20),
    )(remote(mode_weight), local(line))
    rows, mine, other = pl.pallas_call(
        middle_kernel(scale_in, scale_out),
        in_specs=[pl.BlockSpec(memory_space=pltpu.SMEM), vmem, vmem, vmem],
        out_specs=[hbm, vmem, vmem],
        out_shape=[
            pltpu.HBM((128, 8, 256), bf16),
            pltpu.VMEM((2, 16, 8, 128), bf16),
            jax.ShapeDtypeStruct((2, 16, 8, 128), bf16),
        ],
        scratch_shapes=[
            pltpu.VMEM((256, 128), bf16),
            pltpu.VMEM((2, 256, 128), f32),
            pltpu.VMEM((256, 128), f32),
            pltpu.VMEM((128, 8, 256), bf16),
            pltpu.SemaphoreType.DMA((2,)),
        ],
        name="middle",
        compiler_params=pltpu.CompilerParams(vmem_limit_bytes=24 << 20),
    )(core, local(recv), local(weights), local(line))
    back = lax.all_to_all(rows, "gx", split_axis=0, concat_axis=0, tiled=True)
    theirs = lax.ppermute(other, "sa", [(0, 1), (1, 0)])
    mode_grad = pl.pallas_call(
        mode_kernel,
        in_specs=[vmem, vmem],
        out_specs=vmem,
        out_shape=jax.ShapeDtypeStruct((16, 16, 8, 128), f32),
        scratch_shapes=[pltpu.VMEM((2, 16, 8, 128), f32), pltpu.VMEM((2, 16, 8, 128), f32)],
        name="modes",
        compiler_params=pltpu.CompilerParams(vmem_limit_bytes=24 << 20),
    )(local(mine), local(theirs))
    input_grad = pl.pallas_call(
        inverse_kernel(scale_in),
        in_specs=[vmem, vmem, vmem, hbm],
        out_specs=hbm,
        out_shape=jax.ShapeDtypeStruct(field, bf16),
        scratch_shapes=[
            pltpu.VMEM((4, 512, 128), f32),
            pltpu.VMEM(field, f32),
            pltpu.VMEM(field, bf16),
            pltpu.SemaphoreType.DMA((4,)),
            pltpu.SemaphoreType.DMA((4,)),
        ],
        name="inverse",
        compiler_params=pltpu.CompilerParams(vmem_limit_bytes=24 << 20),
    )(local(back), local(plane_back), local(time_inverse), remote(bypass))
    return (input_grad[None], mode_grad)


def solution(mesh):
    field = P("sa", None, "gx", None, None)
    return jax.shard_map(
        shards,
        mesh=mesh,
        in_specs=(field, field, field, P(None, None, "gx", None), P()),
        out_specs=(field, P(None, None, ("gx", "sa"), None)),
        check_vma=False,
    )
```

```python
import math

import jax
import jax.numpy as jnp
import numpy as np
from jax import lax
from jax.experimental import pallas as pl
from jax.experimental.pallas import tpu as pltpu
from jax.sharding import PartitionSpec as P

MY = 64
MT = 32

root_half = math.sqrt(0.5)
gauss_norm = 1.0 / math.sqrt(2.0 * math.pi)
f32 = jnp.float32
bf16 = jnp.bfloat16


def tables(kept_count, length, two_sided):
    frequency = np.arange(kept_count)
    if two_sided:
        frequency = np.where(
            frequency < kept_count // 2, frequency, frequency + (length - kept_count)
        )
    product = frequency[:, None] * np.arange(length)[None, :] % length
    phase_angle = product * (2.0 * math.pi / length)
    return (
        np.cos(phase_angle).astype(np.float32).astype(bf16).astype(np.float32),
        np.sin(phase_angle).astype(np.float32).astype(bf16).astype(np.float32),
    )


def constants(cells_x, cells_y, cells_time, modes_x, slab):
    ct, st = tables(MT, cells_time, False)
    cy, sy = tables(MY, cells_y, True)
    cx, sx = tables(modes_x, cells_x, True)
    four = np.eye(4, dtype=np.float32)
    time = np.stack([ct, -st]).reshape(2, 2, MT // 2, cells_time)
    time_forward = np.einsum("cd,qhkt->ctqhdk", four, time).reshape(4 * cells_time, -1)
    time_inverse = np.einsum("cd,qhkt->qhckdt", four, time).reshape(-1, 4 * cells_time)
    plane = np.block([[cy, sy], [-sy, cy]])
    plane_rows = plane.reshape(2, MY, 1, -1).repeat(2, 2).transpose(1, 2, 0, 3)
    plane_rows = plane_rows.reshape(MY * 4, -1)
    line = np.stack([np.concatenate([cx, -sx]), np.concatenate([sx, cx])], -1)
    line = line.reshape(2 * modes_x, -1).T
    return [
        a.astype(bf16) for a in (time_forward, time_inverse, plane_rows, plane.T, line)
    ]


def low_lanes(shape):
    return lax.broadcasted_iota(jnp.int32, shape, len(shape) - 1) < 64


def gelu_backward(values, cotangent):
    scaled = values * root_half
    density = jnp.exp2((scaled * scaled) * -math.log2(math.e))
    slope = (1.0 + lax.erf(scaled)) + (scaled * (4.0 * root_half * gauss_norm)) * density
    return (cotangent * 0.5) * slope


def forward_kernel(
    pre_hbm,
    cot_hbm,
    inp_hbm,
    time_hbm,
    plane_hbm,
    send_hbm,
    dz_ref,
    pre_ref,
    cot_ref,
    inp_ref,
    time_ref,
    plane_ref,
    send_ref,
    table_ref,
    sect_ref,
    half_ref,
    sems,
    table_sems,
    sent,
):
    plane_copy = pltpu.make_async_copy(plane_hbm, plane_ref, table_sems.at[0])
    time_copy = pltpu.make_async_copy(time_hbm, time_ref, table_sems.at[1])
    plane_copy.start()
    time_copy.start()
    copies = []
    for g in range(4):
        part = pl.ds(4 * g, 4)
        trio = [
            pltpu.make_async_copy(src.at[part], dst.at[part], sems.at[n, g])
            for n, (src, dst) in enumerate(
                ((inp_hbm, inp_ref), (pre_hbm, pre_ref), (cot_hbm, cot_ref))
            )
        ]
        for copy in trio:
            copy.start()
        copies.append(trio)
    row_x = lax.broadcasted_iota(jnp.int32, (256, 256), 0) // 2 % 2
    plane_copy.wait()
    plane = plane_ref[...].astype(f32)
    for x in range(2):
        table_ref[:, 256 * x : 256 * x + 256] = jnp.where(row_x == x, plane, 0.0).astype(bf16)
    top = lax.broadcasted_iota(jnp.int32, (32, 8, 128), 1) < 4
    low = low_lanes((256, 128))
    time_copy.wait()

    def arrive(g):
        for copy in copies[g]:
            copy.wait()

    def activation(g):
        for c in range(4 * g, 4 * g + 4):
            for x in range(4):
                dz_ref[c, x] = gelu_backward(
                    pre_ref[c, x].astype(f32), cot_ref[c, x].astype(f32)
                ).astype(bf16)

    def along_time(field, g):
        ref = (dz_ref, inp_ref)[field]
        rows = jnp.concatenate([ref[4 * g + c].reshape(512, 128) for c in range(4)], axis=1)
        sect = jnp.dot(rows, time_ref[...], preferred_element_type=f32).astype(bf16)
        side = g % 2
        for x in range(4):
            for q in range(2):
                sect_ref[
                    field,
                    256 * x + 128 * q : 256 * x + 128 * q + 128,
                    128 * side : 128 * side + 128,
                ] = sect[128 * x : 128 * x + 128, 128 * q : 128 * q + 128]

    def along_y(field):
        parts = []
        for pair in range(2):
            spectra = jnp.dot(
                table_ref[...],
                sect_ref[field, 512 * pair : 512 * pair + 512, :],
                preferred_element_type=f32,
            )
            first, second = spectra[:, :128], spectra[:, 128:]
            parts.append(
                (
                    jnp.where(low, first, pltpu.roll(second, 64, 1)).reshape(32, 8, 128),
                    jnp.where(low, pltpu.roll(first, 64, 1), second).reshape(32, 8, 128),
                )
            )
        halves = []
        for h in range(2):
            one, two = parts[0][h], parts[1][h]
            even = jnp.where(top, one, pltpu.roll(two, 4, 1))
            odd = jnp.where(top, pltpu.roll(one, 4, 1), two)
            halves.append(jnp.stack([even, odd], axis=1).reshape(64, 8, 128))
        return halves

    def hold(halves):
        for h in range(2):
            half_ref[h] = halves[h]

    def send(pair, halves):
        for h in range(2):
            both = jnp.concatenate([halves[h], half_ref[h]], axis=1)
            send_ref[:, h, :, 128 * pair : 128 * pair + 128] = both.astype(bf16)
        lanes = (slice(None), slice(None), slice(None), pl.ds(128 * pair, 128))
        copy = pltpu.make_async_copy(send_ref.at[lanes], send_hbm.at[lanes], sent.at[pair])
        copy.start()
        return copy

    for g in range(4):
        arrive(g)
    along_time(1, 0)
    activation(0)
    along_time(1, 1)
    along_time(0, 0)
    activation(1)
    hold(along_y(1))
    along_time(0, 1)
    activation(2)
    first = send(0, along_y(0))
    along_time(1, 2)
    along_time(1, 3)
    along_time(0, 2)
    activation(3)
    hold(along_y(1))
    along_time(0, 3)
    second = send(1, along_y(0))
    first.wait()
    second.wait()


def middle_kernel(scale_in, scale_out):
    def kernel(
        core_ref,
        recv_ref,
        w_ref,
        xi_ref,
        send_hbm,
        mine_ref,
        other_ref,
        back_ref,
        g_ref,
        gr_ref,
        send_ref,
        sent,
    ):
        core = core_ref[0]
        line = xi_ref[...].T
        block = recv_ref[...].astype(f32)
        hats = []
        for f, scale in enumerate((scale_out, scale_in)):
            rows = block[:, 8 * f : 8 * f + 8, :].reshape(1024, 256).astype(bf16)
            summed = jnp.dot(line, rows, preferred_element_type=f32)
            hats.append((scale * summed).T.astype(bf16).astype(f32))
        grad = hats[0]
        g_ref[0] = grad
        g_ref[1] = hats[1]
        gr_ref[...] = pltpu.roll(grad, 64, 1)
        for f in range(2):
            for c in range(16):
                mine_ref[f, c] = g_ref[f, pl.ds(16 * c + 8 * core, 8), :].astype(bf16)
                other_ref[f, c] = g_ref[f, pl.ds(16 * c + 8 - 8 * core, 8), :].astype(bf16)
        low = low_lanes((16, 128))
        for i in range(16):
            same = jnp.zeros((16, 128), f32)
            cross = jnp.zeros((16, 128), f32)
            for o in range(16):
                weight = w_ref[i, o].astype(f32)
                same = same + weight * g_ref[0, 16 * o : 16 * o + 16, :]
                cross = cross + weight * gr_ref[16 * o : 16 * o + 16, :]
            back = jnp.where(low, same + pltpu.roll(same, 64, 1), pltpu.roll(cross, 64, 1) - cross)
            back_ref[16 * i : 16 * i + 16, :] = back.astype(bf16)
        copies = []
        for part in range(2):
            grid_rows = lax.dot_general(
                xi_ref[512 * part : 512 * part + 512],
                back_ref[...],
                (((1,), (1,)), ((), ())),
                preferred_element_type=f32,
            )
            block = pl.ds(64 * part, 64)
            send_ref[block] = grid_rows.reshape(64, 8, 256).astype(bf16)
            copies.append(
                pltpu.make_async_copy(send_ref.at[block], send_hbm.at[block], sent.at[part])
            )
            copies[-1].start()
        for copy in copies:
            copy.wait()

    return kernel


def mode_kernel(mine_ref, other_ref, out_ref, g_ref, gx_ref):
    low = low_lanes((16, 8, 128))
    for s, ref in enumerate((mine_ref, other_ref)):
        grad = ref[0].astype(f32)
        rolled = pltpu.roll(grad, 64, 2)
        g_ref[s] = grad
        gx_ref[s] = jnp.where(low, rolled, -rolled)
    low = low_lanes((8, 128))
    for i in range(16):
        real, imag = [], []
        for ref in (mine_ref, other_ref):
            value = ref[1, i].astype(f32)
            rolled = pltpu.roll(value, 64, 1)
            real.append(jnp.where(low, value, rolled))
            imag.append(jnp.where(low, rolled, value))
        for o in range(16):
            out_ref[i, o] = (
                real[0] * g_ref[0, o]
                + imag[0] * gx_ref[0, o]
                + (real[1] * g_ref[1, o] + imag[1] * gx_ref[1, o])
            )


def bypass_kernel(
    b_ref, dz_ref, xi_hbm, out_hbm, xi_ref, out_ref, sems, sent
):
    copies = [
        pltpu.make_async_copy(src, dst, sems.at[n])
        for n, (src, dst) in enumerate(((xi_hbm, xi_ref),))
    ]
    for copy in copies:
        copy.start()
    row = lax.broadcasted_iota(jnp.int32, (256, 16), 0)
    col = lax.broadcasted_iota(jnp.int32, (256, 16), 1)
    spread = jnp.where(row // 16 == col, 1.0, 0.0).astype(bf16)
    left = jnp.dot(spread, b_ref[...], preferred_element_type=f32).astype(bf16)
    full = lax.dot_general(left, spread, (((1,), (1,)), ((), ())), preferred_element_type=f32)
    row = lax.broadcasted_iota(jnp.int32, (256, 256), 0)
    col = lax.broadcasted_iota(jnp.int32, (256, 256), 1)
    mix = jnp.where(row % 16 == col % 16, full, 0.0).astype(bf16)
    def cell(x, carry):
        rows = jnp.concatenate(
            [
                jnp.concatenate([dz_ref[o, x, 16 * b : 16 * b + 16, :] for o in range(16)], axis=0)
                for b in range(8)
            ],
            axis=1,
        )
        mixed = jnp.dot(mix, rows, preferred_element_type=f32)
        for i in range(16):
            for b in range(8):
                out_ref[i, x, 16 * b : 16 * b + 16, :] = mixed[
                    16 * i : 16 * i + 16, 128 * b : 128 * b + 128
                ]
        return carry

    lax.fori_loop(0, 4, cell, 0)
    copies.append(pltpu.make_async_copy(out_ref, out_hbm, sent))
    copies[-1].start()
    for copy in copies:
        copy.wait()


def fetch_kernel(w_hbm, after_ref, w_ref, sem):
    copy = pltpu.make_async_copy(w_hbm, w_ref, sem)
    copy.start()
    copy.wait()


def inverse_kernel():
    def kernel(recv_ref, plane_ref, time_ref, bypass_hbm, out_hbm, rows_ref, bypass_ref, out_ref, loads, sems):
        arriving = [
            pltpu.make_async_copy(bypass_hbm.at[:, x], bypass_ref.at[:, x], loads.at[x])
            for x in range(4)
        ]
        for copy in arriving:
            copy.start()
        block = recv_ref[...].astype(f32).reshape(64, 2, 8, 256)
        low = low_lanes((512, 128))
        for v in range(2):
            first = block[:, 0, :, 128 * v : 128 * v + 128].reshape(512, 128)
            second = block[:, 1, :, 128 * v : 128 * v + 128].reshape(512, 128)
            rows_ref[2 * v] = jnp.where(low, first, pltpu.roll(second, 64, 1))
            rows_ref[2 * v + 1] = jnp.where(low, pltpu.roll(first, 64, 1), second)
        copies = []
        for x in range(4):
            spectra = jnp.concatenate(
                [
                    jnp.concatenate(
                        [rows_ref[g, pl.ds(2 * x + a, 64, stride=8), :] for a in range(2)], axis=0
                    )
                    for g in range(4)
                ],
                axis=1,
            ).astype(bf16)
            joined = jnp.dot(plane_ref[...], spectra, preferred_element_type=f32).astype(bf16)
            stacked = jnp.concatenate(
                [
                    jnp.concatenate(
                        [
                            joined[128 * q : 128 * q + 128, 128 * g : 128 * g + 128]
                            for q in range(2)
                        ],
                        axis=1,
                    )
                    for g in range(4)
                ],
                axis=0,
            )
            arriving[x].wait()
            spectral = jnp.dot(stacked, time_ref[...], preferred_element_type=f32)
            for g in range(4):
                for c in range(4):
                    out_ref[4 * g + c, x] = (
                        spectral[128 * g : 128 * g + 128, 128 * c : 128 * c + 128]
                        + bypass_ref[4 * g + c, x]
                    ).astype(bf16)
            copies.append(
                pltpu.make_async_copy(out_ref.at[:, x], out_hbm.at[:, x], sems.at[x])
            )
            copies[-1].start()
        for copy in copies:
            copy.wait()

    return kernel


def remote(array):
    return pltpu.with_memory_space_constraint(array, pltpu.HBM)


def local(array):
    return pltpu.with_memory_space_constraint(array, pltpu.VMEM)


def shards(inputs, preact, cotangent, mode_weight, bypass_weight):
    slab = inputs.shape[2]
    cells_y = inputs.shape[3]
    cells_time = inputs.shape[4]
    cells_x = slab * lax.axis_size("gx")
    modes_x = mode_weight.shape[3] // 2
    cell_count = cells_x * cells_y * cells_time
    scale_in = float(modes_x * MY * MT * cell_count) ** (-0.25)
    scale_out = float(cell_count) ** (-0.5)
    time_forward, time_inverse, plane, plane_back, line = constants(
        cells_x, cells_y, cells_time, modes_x, slab
    )
    assert math.frexp(scale_in)[0] == 0.5
    time_inverse = (time_inverse.astype(np.float32) * scale_in).astype(bf16)
    core = lax.axis_index("sa").astype(jnp.int32).reshape(1)

    vmem = pl.BlockSpec(memory_space=pltpu.VMEM)
    hbm = pl.BlockSpec(memory_space=pltpu.HBM)
    field = (16, 4, 128, 128)
    send, dz = pl.pallas_call(
        forward_kernel,
        in_specs=[hbm] * 5,
        out_specs=[hbm, vmem],
        out_shape=[pltpu.HBM((64, 2, 16, 256), bf16), pltpu.VMEM(field, bf16)],
        scratch_shapes=[pltpu.VMEM(field, bf16)] * 3
        + [
            pltpu.VMEM(time_forward.shape, bf16),
            pltpu.VMEM(plane.shape, bf16),
            pltpu.VMEM((64, 2, 16, 256), bf16),
            pltpu.VMEM((256, 512), bf16),
            pltpu.VMEM((2, 1024, 256), bf16),
            pltpu.VMEM((2, 64, 8, 128), f32),
            pltpu.SemaphoreType.DMA((3, 4)),
            pltpu.SemaphoreType.DMA((2,)),
            pltpu.SemaphoreType.DMA((2,)),
        ],
        name="forward",
        compiler_params=pltpu.CompilerParams(vmem_limit_bytes=24 << 20),
    )(
        remote(preact[0]),
        remote(cotangent[0]),
        remote(inputs[0]),
        remote(time_forward),
        remote(plane),
    )
    recv = lax.all_to_all(
        send.reshape(128, 16, 256), "gx", split_axis=0, concat_axis=0, tiled=True
    )
    bypass, line = pl.pallas_call(
        bypass_kernel,
        in_specs=[vmem, vmem, hbm],
        out_specs=[hbm, vmem],
        out_shape=[
            pltpu.HBM(field, f32),
            pltpu.VMEM(line.shape, bf16),
        ],
        scratch_shapes=[
            pltpu.VMEM(field, f32),
            pltpu.SemaphoreType.DMA((1,)),
            pltpu.SemaphoreType.DMA,
        ],
        name="bypass",
        compiler_params=pltpu.CompilerParams(vmem_limit_bytes=24 << 20),
    )(bypass_weight, local(dz), remote(line))
    weights = pl.pallas_call(
        fetch_kernel,
        in_specs=[hbm, vmem],
        out_specs=vmem,
        out_shape=pltpu.VMEM(mode_weight.shape, bf16),
        scratch_shapes=[pltpu.SemaphoreType.DMA],
        name="fetch",
        compiler_params=pltpu.CompilerParams(vmem_limit_bytes=24 << 20),
    )(remote(mode_weight), local(line))
    rows, mine, other = pl.pallas_call(
        middle_kernel(scale_in, scale_out),
        in_specs=[pl.BlockSpec(memory_space=pltpu.SMEM), vmem, vmem, vmem],
        out_specs=[hbm, vmem, vmem],
        out_shape=[
            pltpu.HBM((128, 8, 256), bf16),
            pltpu.VMEM((2, 16, 8, 128), bf16),
            jax.ShapeDtypeStruct((2, 16, 8, 128), bf16),
        ],
        scratch_shapes=[
            pltpu.VMEM((256, 128), bf16),
            pltpu.VMEM((2, 256, 128), f32),
            pltpu.VMEM((256, 128), f32),
            pltpu.VMEM((128, 8, 256), bf16),
            pltpu.SemaphoreType.DMA((2,)),
        ],
        name="middle",
        compiler_params=pltpu.CompilerParams(vmem_limit_bytes=24 << 20),
    )(core, local(recv), local(weights), local(line))
    back = lax.all_to_all(rows, "gx", split_axis=0, concat_axis=0, tiled=True)
    theirs = lax.ppermute(other, "sa", [(0, 1), (1, 0)])
    mode_grad = pl.pallas_call(
        mode_kernel,
        in_specs=[vmem, vmem],
        out_specs=vmem,
        out_shape=jax.ShapeDtypeStruct((16, 16, 8, 128), f32),
        scratch_shapes=[pltpu.VMEM((2, 16, 8, 128), f32), pltpu.VMEM((2, 16, 8, 128), f32)],
        name="modes",
        compiler_params=pltpu.CompilerParams(vmem_limit_bytes=24 << 20),
    )(local(mine), local(theirs))
    input_grad = pl.pallas_call(
        inverse_kernel(),
        in_specs=[vmem, vmem, vmem, hbm],
        out_specs=hbm,
        out_shape=jax.ShapeDtypeStruct(field, bf16),
        scratch_shapes=[
            pltpu.VMEM((4, 512, 128), f32),
            pltpu.VMEM(field, f32),
            pltpu.VMEM(field, bf16),
            pltpu.SemaphoreType.DMA((4,)),
            pltpu.SemaphoreType.DMA((4,)),
        ],
        name="inverse",
        compiler_params=pltpu.CompilerParams(vmem_limit_bytes=24 << 20),
    )(local(back), local(plane_back), local(time_inverse), remote(bypass))
    return (input_grad[None], mode_grad)


def solution(mesh):
    field = P("sa", None, "gx", None, None)
    return jax.shard_map(
        shards,
        mesh=mesh,
        in_specs=(field, field, field, P(None, None, "gx", None), P()),
        out_specs=(field, P(None, None, ("gx", "sa"), None)),
        check_vma=False,
    )
```
